32 devices in a mesh: row: 8 (over z, x), col: 4 (over y, core).
Axes of the slice: x: 2, y: 2, z: 4, core: 2. Of those that a mesh axis runs over, the one named last changes fastest.
Arguments:
- obj_re: float32 [1024, 512], P('row', 'col'), may hold values from -6 to 6
- obj_im: float32 [1024, 512], P('row', 'col'), may hold values from -6 to 6
- probe_re: float32 [4, 256, 256], replicated, may hold values from -3 to 3
- probe_im: float32 [4, 256, 256], replicated, may hold values from -3 to 3
- amps: float32 [8, 4, 1, 256, 256], P('row', 'col'), may hold values from 0.2 to 4
- positions: int32 [8, 4, 1, 2], P('row', 'col'), may hold values from -128 to 896, as said below
Outputs:
- new_obj_re: float32 [1024, 512], P('row', 'col')
- new_obj_im: float32 [1024, 512], P('row', 'col')
- new_probe_re: float32 [4, 256, 256], replicated
- new_probe_im: float32 [4, 256, 256], replicated
The draws below stay inside these ranges and needn't reach their ends.
Inputs may be any that keep to these rules, and one draw needn't show every extreme that they name: `positions`: each position's offsets are multiples of 64. A position stored at [i, j, p] has its row r with i * 128 - 256 // 2 <= r <= (i + 1) * 128 - 256 // 2 and its column c with j * 128 - 256 // 2 <= c <= (j + 1) * 128 - 256 // 2.
All inputs are finite; a program needn't handle non-finite values.
Results may differ from the reference program's by a relative error of at most 0.0055.
Values sent between devices are 32-bit elements; how exact they have to be, the bound alone decides.
No kernel may reach another device: no remote copies, remote signals or barrier semaphores. Data moves between devices by JAX's collectives and lax.ppermute only.
A program may use at most 64 MiB of HBM per device.

```python
import math
import jax
import jax.numpy as jnp
from jax import lax

W = 256
MODES = 4
ITERS = 3
TR = 128
TC = 128
POS_DEV = 1
NR = 1024
NC = 512
N_ROW = 8
N_COL = 4


def draw_positions(key, part):
    first_key = jax.random.fold_in(key, 11)
    second_key = jax.random.fold_in(key, 23)
    step = W // 4
    row_ids = jnp.arange(N_ROW, dtype=jnp.int32)[:, None, None]
    col_ids = jnp.arange(N_COL, dtype=jnp.int32)[None, :, None]
    slot_ids = jnp.arange(POS_DEV, dtype=jnp.int32)[None, None, :]
    row_steps = jax.random.randint(first_key, (N_ROW, N_COL, POS_DEV), -2, TR // step - 1)
    col_steps = jax.random.randint(second_key, (N_ROW, N_COL, POS_DEV), -2, TC // step - 1)
    pinned = slot_ids == 0
    first_tile = (row_ids == 0) & (col_ids == 0) & pinned
    last_tile = (row_ids == N_ROW - 1) & (col_ids == N_COL - 1) & pinned
    col_steps = jnp.where(first_tile, -2, jnp.where(last_tile, TC // step - 2, col_steps))
    row_steps = jnp.where(last_tile, TR // step - 2, row_steps)
    rows_at = row_ids * TR + row_steps * step
    cols_at = col_ids * TC + col_steps * step
    return jnp.stack([rows_at, cols_at], axis=-1).astype(jnp.int32)


def block_levels(rng, extent, split, least, largest):
    loudness, own = 1.0, jax.random.fold_in(rng, 6)
    for axis_at, blocks in split:
        heights = jnp.exp(jax.random.uniform(jax.random.fold_in(own, axis_at), (blocks,), jnp.float32, least / len(split), largest / len(split)))
        loudness = loudness * jnp.repeat(heights, extent[axis_at] // blocks).reshape([-1 if axis == axis_at else 1 for axis in range(len(extent))])
    return loudness


def centred(rng, dims, scale, reach, split=(), kind=jnp.bfloat16):
    factor_of = block_levels(rng, dims, split, -0.22, 0.18) if split else 1.0
    result = jax.random.normal(rng, dims, jnp.float32) * scale * factor_of
    return jnp.minimum(jnp.maximum(result, -reach), reach).astype(kind)


def setup_inputs(seed: int = 0) -> dict:
    key_list = jax.random.split(jax.random.key(seed), 7)
    return {
        "obj_re": centred(key_list[0], (NR, NC), 1.0, 6.0, ((0, 8), (1, 4)), jnp.float32),
        "obj_im": centred(key_list[1], (NR, NC), 1.0, 6.0, ((0, 8), (1, 4)), jnp.float32),
        "probe_re": centred(key_list[2], (MODES, W, W), 0.5, 3.0, (), jnp.float32),
        "probe_im": centred(key_list[3], (MODES, W, W), 0.5, 3.0, (), jnp.float32),
        "amps": jnp.clip(0.2 + 3.8 * jax.random.uniform(key_list[4], (N_ROW, N_COL, POS_DEV, W, W), jnp.float32) ** block_levels(key_list[4], (N_ROW, N_COL, POS_DEV, W, W), ((0, 8), (1, 4)), -0.2, 0.2), 0.2, 4.0),
        "positions": draw_positions(jax.random.fold_in(key_list[6], 71), 0),
    }


amp_floor = 0.25
light_ratio = 0.1
mass_ratio = 0.1
probe_step = 6.0

def make_tables(width, sign):
    index = jnp.arange(width, dtype=jnp.int32)
    turns = index[:, None] * index[None, :] % width
    angle = turns.astype(jnp.float32) * (2.0 * math.pi / width)
    real = (jnp.cos(angle) / math.sqrt(width)).astype(jnp.bfloat16)
    imag = (sign * jnp.sin(angle) / math.sqrt(width)).astype(jnp.bfloat16)
    right_pair = jnp.concatenate([jnp.concatenate([real, imag], 1), jnp.concatenate([-imag, real], 1)], 0)
    return (right_pair, real, imag)

def transform(wave, table):
    right_pair, real, imag = table
    width = real.shape[0]
    half = jnp.einsum('mnc,cd->mnd', wave.astype(jnp.float32), right_pair.astype(jnp.float32)).astype(jnp.bfloat16)
    first = jnp.einsum('kn,mnd->mkd', real.astype(jnp.float32), half.astype(jnp.float32))
    second = jnp.einsum('kn,mnd->mkd', imag.astype(jnp.float32), half.astype(jnp.float32))
    return (first[..., :width] - second[..., width:], first[..., width:] + second[..., :width])

def one_view(window, probe_re, probe_im, view, forward, backward):
    win_re = window[0][None]
    win_im = window[1][None]
    psi = jnp.concatenate([probe_re * win_re - probe_im * win_im, probe_re * win_im + probe_im * win_re], axis=2).astype(jnp.bfloat16)
    spec_re, spec_im = transform(psi, forward)
    modulus = jnp.sqrt(lax.optimization_barrier(jnp.sum(spec_re * spec_re + spec_im * spec_im, axis=0)))
    factor = view / jnp.maximum(modulus, amp_floor) - 1.0
    change = jnp.concatenate([spec_re * factor, spec_im * factor], axis=2).astype(jnp.bfloat16)
    return transform(change, backward)

def place(buffer, piece, row_at, col_at):
    start = (jnp.int32(0), row_at, col_at)
    current = lax.dynamic_slice(buffer, start, piece.shape)
    return lax.dynamic_update_slice(buffer, current + piece, start)

def reference(obj_re, obj_im, probe_re, probe_im, amps, positions):
    rim = W // 2
    forward = make_tables(W, -1.0)
    backward = make_tables(W, 1.0)
    spots = positions.reshape(-1, 2).astype(jnp.int32)
    views = amps.reshape(-1, W, W)
    power = lax.optimization_barrier(jnp.sum(probe_re * probe_re + probe_im * probe_im, axis=0))
    big_rows = NR + 2 * rim
    big_cols = NC + 2 * rim

    def add_light(buffer, spot):
        return (place(buffer, power[None], spot[0] + rim, spot[1] + rim), None)
    light_buf, unused = lax.scan(add_light, jnp.zeros((1, big_rows, big_cols), jnp.float32), spots)
    light = light_buf[0, rim:rim + NR, rim:rim + NC]
    denom = light + light_ratio * jnp.max(light)
    state = jnp.stack([obj_re, obj_im])
    probe_grad = None
    for step in range(ITERS):
        padded = jnp.pad(state, ((0, 0), (rim, rim), (rim, rim)))

        def visit(carry, item):
            buffer, grad_re, grad_im, mass = carry
            spot, view = item
            window = lax.dynamic_slice(padded, (jnp.int32(0), spot[0] + rim, spot[1] + rim), (2, W, W))
            exit_re, exit_im = one_view(window, probe_re, probe_im, view, forward, backward)
            obj_grad = jnp.stack([lax.optimization_barrier(jnp.sum(probe_re * exit_re + probe_im * exit_im, axis=0)), lax.optimization_barrier(jnp.sum(probe_re * exit_im - probe_im * exit_re, axis=0))])
            buffer = place(buffer, obj_grad, spot[0] + rim, spot[1] + rim)
            win_re = window[0][None]
            win_im = window[1][None]
            grad_re = grad_re + win_re * exit_re + win_im * exit_im
            grad_im = grad_im + win_re * exit_im - win_im * exit_re
            mass = mass + window[0] * window[0] + window[1] * window[1]
            return ((buffer, grad_re, grad_im, mass), None)
        init = (jnp.zeros((2, big_rows, big_cols), jnp.float32), jnp.zeros((MODES, W, W), jnp.float32), jnp.zeros((MODES, W, W), jnp.float32), jnp.zeros((W, W), jnp.float32))
        (buffer, grad_re, grad_im, mass), unused = lax.scan(visit, init, (spots, views))
        probe_grad = (grad_re, grad_im, mass)
        state = state + buffer[:, rim:rim + NR, rim:rim + NC] / denom[None]
    grad_re, grad_im, mass = probe_grad
    scale = probe_step / (mass + mass_ratio * jnp.mean(mass))
    return (state[0], state[1], probe_re + grad_re * scale[None], probe_im + grad_im * scale[None])
```

```python
import functools
import math

import jax
import jax.numpy as jnp
import numpy as np
from jax import lax
from jax.experimental import pallas as pl
from jax.experimental.pallas import tpu as pltpu
from jax.sharding import PartitionSpec as P

ITERS = 3

amp_floor = 0.25
light_ratio = 0.1
mass_ratio = 0.1
probe_step = 6.0

F32 = jnp.float32
BF16 = jnp.bfloat16
KEEP_ROWS = 16
HEAD = 2


def tables(width):
    index = np.arange(width)
    angle = (index[:, None] * index[None, :] % width) * (2.0 * math.pi / width)
    real = (np.cos(angle) / math.sqrt(width)).astype(np.float32)
    imag = (-np.sin(angle) / math.sqrt(width)).astype(np.float32)
    right = np.block([[real, imag], [-imag, real]]).astype(BF16)
    left = np.block([[real, -imag], [imag, real]]).astype(BF16)
    return right, left


def near_pairs(count):
    return [(i, i ^ 1) for i in range(count)]


def far_pairs(count):
    return [(i, (i + 1 if i % 2 else i - 1) % count) for i in range(count)]


def swap_near(array, axis):
    return lax.ppermute(array, axis, near_pairs(lax.axis_size(axis)))


def swap_far(array, axis):
    return lax.ppermute(array, axis, far_pairs(lax.axis_size(axis)))


def call(body, outs, scratch=(), smem=1, limit=None, cost=None):
    def run(*args):
        specs = [pl.BlockSpec(memory_space=pltpu.SMEM)] * smem
        specs += [pl.BlockSpec(memory_space=pltpu.VMEM)] * (len(args) - smem)
        return pl.pallas_call(
            body,
            out_shape=[jax.ShapeDtypeStruct(s, F32) for s in outs],
            in_specs=specs,
            out_specs=[pl.BlockSpec(memory_space=pltpu.VMEM)] * len(outs),
            scratch_shapes=list(scratch),
            compiler_params=pltpu.CompilerParams(vmem_limit_bytes=limit),
            cost_estimate=cost,
        )(*args)

    return run


class Place:
    def __init__(self, sc, sizes):
        n_row, n_col, rows, cols, rim = sizes
        self.i, self.j = sc[0], sc[1]
        self.even_row = self.i % 2 == 0
        self.even_col = self.j % 2 == 0
        self.up = self.i > 0
        self.down = self.i < n_row - 1
        self.has_left = self.j > 0
        self.has_right = self.j < n_col - 1
        self.far_row = jnp.where(self.even_row, self.i, n_row - 1 - self.i) > 0
        self.far_col = jnp.where(self.even_col, self.j, n_col - 1 - self.j) > 0
        near = jnp.where(self.even_col, self.j + 1, self.j - 1)
        far = jnp.where(self.even_col, self.j - 1, self.j + 1)
        far = jnp.where(self.far_col, far, self.j)

        def row_of(col):
            at = sc[HEAD + 2 * (self.i * n_col + col)]
            return pl.multiple_of(at - (self.i * rows - rim), rim // 2)

        self.row = row_of(self.j)
        self.near_row = row_of(near)
        self.far_row_at = row_of(far)
        self.col = sc[HEAD + 2 * (self.i * n_col + self.j) + 1] - (self.j * cols - rim)


def light_body(sizes, n_dev, sc, pr, pi, out, buf, pw):
    n_row, n_col, rows, cols, rim = sizes
    width = 2 * rim
    half = rim // 2
    power = jnp.sum(pr[...] * pr[...] + pi[...] * pi[...], axis=0)
    lane = lax.broadcasted_iota(jnp.int32, (width, rim), 1)
    a, b = power[:, :rim], power[:, rim:]
    ra, rb = pltpu.roll(a, half, 1), pltpu.roll(b, half, 1)
    zero = jnp.zeros((width, rim), F32)
    pw[0] = jnp.concatenate([a, b, zero], axis=1)
    pw[1] = jnp.concatenate(
        [jnp.where(lane < half, 0.0, ra), jnp.where(lane < half, ra, rb), jnp.where(lane < half, rb, 0.0)],
        axis=1,
    )
    buf[...] = jnp.zeros_like(buf)

    def add(p, carry):
        row = pl.multiple_of(sc[HEAD + 2 * p] + rim, half)
        col = sc[HEAD + 2 * p + 1] + rim
        odd = (col // half) % 2
        at = (pl.ds(row, width), pl.ds(pl.multiple_of(col - odd * half, rim), width + rim))
        buf[at] += pw[odd]
        return carry

    lax.fori_loop(0, n_dev, add, 0)

    def peak_of(k, best):
        at = pl.multiple_of(k * rows + rim, rim)
        return jnp.maximum(best, jnp.max(buf[pl.ds(at, rows), rim : rim + n_col * cols]))

    peak = lax.fori_loop(0, n_row, peak_of, jnp.float32(0.0))
    mine = buf[
        pl.ds(pl.multiple_of(sc[0] * rows + rim, rim), rows),
        pl.ds(pl.multiple_of(sc[1] * cols + rim, rim), cols),
    ]
    out[...] = mine + light_ratio * peak


def halo_body(sizes, sc, s, near, far, mid, to_near, to_far, ext):
    n_row, n_col, rows, cols, rim = sizes
    at = Place(sc, sizes)
    width = 2 * rim
    above = jnp.where(at.even_row, far[...], near[...])
    below = jnp.where(at.even_row, near[...], far[...])
    ext[:, :rim] = jnp.where(at.up, above, 0.0)
    ext[:, rim : rim + rows] = s[...]
    ext[:, rim + rows :] = jnp.where(at.down, below, 0.0)
    mid[...] = ext[:, pl.ds(at.row, width)]
    to_near[...] = ext[:, pl.ds(at.near_row, width)]
    to_far[...] = ext[:, pl.ds(at.far_row_at, width)]


def view_body(sizes, last, sc, mid, near, far, pr, pi, view, right_t, left_t, *refs):
    if last:
        gm, to_near, to_far, keep, send, spec_scr, win_scr, term_scr = refs
    else:
        gm, to_near, to_far, spec_scr, win_scr = refs
    n_row, n_col, rows, cols, rim = sizes
    at = Place(sc, sizes)
    modes, width = pr.shape[0], pr.shape[1]
    half = rim // 2
    lane = lax.broadcasted_iota(jnp.int32, (width, rim), 1)
    first = at.col == 0
    middle = at.col == half
    for part in range(2):
        a, b = near[part], far[part]
        lft = jnp.where(at.has_left, jnp.where(at.even_col, b, a), 0.0)
        rgt = jnp.where(at.has_right, jnp.where(at.even_col, a, b), 0.0)
        own = mid[part]
        rl, ro, rr = (pltpu.roll(t, half, 1) for t in (lft, own, rgt))
        win_scr[part, :, :rim] = jnp.where(
            first, lft, jnp.where(middle, jnp.where(lane < half, rl, ro), own)
        )
        win_scr[part, :, rim:] = jnp.where(
            first, own, jnp.where(middle, jnp.where(lane < half, ro, rr), rgt)
        )
    total = jnp.zeros((width, width), F32)
    for m in range(modes):
        wr, wi = win_scr[0], win_scr[1]
        psi = jnp.concatenate(
            [pr[m] * wr - pi[m] * wi, pr[m] * wi + pi[m] * wr], axis=1
        ).astype(BF16)
        mixed = jnp.dot(psi, right_t[...], preferred_element_type=F32).astype(BF16)
        tall = jnp.concatenate([mixed[:, :width], mixed[:, width:]], axis=0)
        spec = jnp.dot(left_t[...], tall, preferred_element_type=F32)
        spec_scr[m] = spec
        total = total + (spec[:width] * spec[:width] + spec[width:] * spec[width:])
    factor = view[...] / jnp.maximum(jnp.sqrt(total), amp_floor) - 1.0
    grad = [jnp.zeros((width, width), F32), jnp.zeros((width, width), F32)]
    for m in range(modes):
        change = jnp.concatenate(
            [spec_scr[m, :width] * factor, spec_scr[m, width:] * factor], axis=1
        ).astype(BF16)
        mixed = jnp.dot(change, left_t[...], preferred_element_type=F32).astype(BF16)
        tall = jnp.concatenate([mixed[:, :width], mixed[:, width:]], axis=0)
        back = jnp.dot(right_t[...], tall, preferred_element_type=F32)
        er, ei = back[:width], back[width:]
        grad[0] = grad[0] + (pr[m] * er + pi[m] * ei)
        grad[1] = grad[1] + (pr[m] * ei - pi[m] * er)
        if last:
            wr, wi = win_scr[0], win_scr[1]
            term_scr[m] = wr * er + wi * ei
            term_scr[modes + m] = wr * ei - wi * er
    for part in range(2):
        a, b = grad[part][:, :rim], grad[part][:, rim:]
        ra, rb = pltpu.roll(a, half, 1), pltpu.roll(b, half, 1)
        low = lane < half
        lft = jnp.where(first, a, jnp.where(middle, jnp.where(low, 0.0, ra), 0.0))
        own = jnp.where(first, b, jnp.where(middle, jnp.where(low, ra, rb), a))
        rgt = jnp.where(first, 0.0, jnp.where(middle, jnp.where(low, rb, 0.0), b))
        gm[part] = own
        to_near[part] = jnp.where(at.even_col, rgt, lft)
        to_far[part] = jnp.where(at.even_col, lft, rgt)
    if last:
        wr, wi = win_scr[0], win_scr[1]
        term_scr[2 * modes] = wr * wr + wi * wi
        bit = at.j % 2
        keep[...] = term_scr[:, pl.ds(pl.multiple_of(bit * rim, rim), rim)]
        send[...] = term_scr[:, pl.ds(pl.multiple_of((1 - bit) * rim, rim), rim)]


def fold_body(sizes, sc, gm, near, far, own, to_near, to_far, buf):
    n_row, n_col, rows, cols, rim = sizes
    at = Place(sc, sizes)
    width = 2 * rim
    buf[...] = jnp.zeros_like(buf)
    buf[:, pl.ds(at.row, width)] = gm[...]
    buf[:, pl.ds(at.near_row, width)] += near[...]
    buf[:, pl.ds(at.far_row_at, width)] += jnp.where(at.far_col, far[...], 0.0)
    top, bottom = buf[:, :rim], buf[:, rim + rows :]
    own[...] = buf[:, rim : rim + rows]
    to_near[...] = jnp.where(at.even_row, bottom, top)
    to_far[...] = jnp.where(at.even_row, top, bottom)


def step_body(sizes, sc, s, own, near, far, denom, out):
    at = Place(sc, sizes)
    grad = own[...] + near[...] + jnp.where(at.far_row, far[...], 0.0)
    out[...] = s[...] + grad / denom[...][None]


def bit_of(sc, axis, level):
    return lax.shift_right_logical(sc[axis], level) % 2


def halve_body(levels, height, shared, sc, *refs):
    count = len(levels)
    ins = 1 if shared else count
    cur, got, out = refs[:ins], refs[ins : 2 * ins], refs[2 * ins :]
    for c, (axis, level) in enumerate(levels):
        bit = bit_of(sc, axis, level)
        each = out[2 * c].shape[0]
        for which, offset in ((0, bit * height), (1, (1 - bit) * height)):
            rows = pl.ds(pl.multiple_of(offset, 8), height)
            if shared:
                at = (slice(c * each, (c + 1) * each), rows)
                out[2 * c + which][...] = cur[0][at] + got[0][at]
            else:
                out[2 * c + which][...] = cur[c][:, rows] + got[c][:, rows]


def gather_sum_body(count, sc, *refs):
    cur, got, out = refs[:count], refs[count : 2 * count], refs[2 * count]
    each = cur[0].shape[0]
    for c in range(count):
        out[c * each : (c + 1) * each] = cur[c][...] + got[c][...]


def spread_sum_body(count, sc, cur, got, *out):
    each = out[0].shape[0]
    for c in range(count):
        at = slice(c * each, (c + 1) * each)
        out[c][...] = cur[at] + got[at]


def sum_body(sc, cur, got, out):
    out[...] = cur[...] + got[...]


def join_body(levels, height, shared, sc, *refs):
    count = len(levels)
    cur, got, out = refs[:count], refs[count : 2 * count], refs[2 * count :]
    for c, (axis, level) in enumerate(levels):
        bit = bit_of(sc, axis, level)
        each = cur[c].shape[0]
        for src, offset in ((cur[c], bit * height), (got[c], (1 - bit) * height)):
            rows = pl.ds(pl.multiple_of(offset, 8), height)
            if shared:
                out[0][c * each : (c + 1) * each, rows] = src[...]
            else:
                out[c][:, rows] = src[...]


def probe_body(rim, sc, mine, got, pr, pi, new_re, new_im):
    modes = pr.shape[0]
    pixels = 4 * rim * rim
    bit = sc[1] % 2
    mean = (jnp.sum(mine[2 * modes]) + jnp.sum(got[2 * modes])) / pixels
    for src, offset in ((mine, bit * rim), (got, (1 - bit) * rim)):
        rows = pl.ds(pl.multiple_of(offset, rim), rim)
        scale = probe_step / (src[2 * modes] + mass_ratio * mean)
        for m in range(modes):
            new_re[m, rows] = pr[m, rows] + src[m] * scale
            new_im[m, rows] = pi[m, rows] + src[modes + m] * scale


def swap_bit(array, where):
    axis, level = where
    name = ("row", "col")[axis]
    count = lax.axis_size(name)
    return lax.ppermute(array, name, [(i, i ^ (1 << level)) for i in range(count)])


def sum_terms(sc, keep, send, n_row, n_col):
    parts, height, width = keep.shape
    colors = 3
    each = parts // colors
    row_bits = [(0, k) for k in range(n_row.bit_length() - 1)]
    col_bits = [(1, k) for k in range(1, n_col.bit_length() - 1)]
    rest = []
    while row_bits or col_bits:
        if row_bits:
            rest.append(row_bits.pop(0))
        if col_bits:
            rest.append(col_bits.pop(0))
    turn = rest[:colors]
    orders = [turn[c:] + turn[:c] for c in range(colors)]
    tail = rest[colors:]
    got = swap_bit(send, (1, 0))
    curs, gots, shared = [keep], [got], True
    steps = []
    for r in range(len(turn)):
        levels = [orders[c][r] for c in range(colors)]
        height //= 2
        outs = [(each, height, width)] * (2 * colors)
        res = call(functools.partial(halve_body, levels, height, shared), outs)(sc, *curs, *gots)
        curs, sends = res[0::2], res[1::2]
        gots = [swap_bit(a, w) for a, w in zip(sends, levels)]
        shared = False
        steps.append(levels)
    (cur,) = call(functools.partial(gather_sum_body, colors), [(parts, height, width)])(
        sc, *curs, *gots
    )
    for where in tail[:-1]:
        got = swap_bit(cur, where)
        (cur,) = call(sum_body, [cur.shape])(sc, cur, got)
    got = swap_bit(cur, tail[-1])
    curs = call(functools.partial(spread_sum_body, colors), [(each, height, width)] * colors)(
        sc, cur, got
    )
    for levels in reversed(steps):
        gots = [swap_bit(a, w) for a, w in zip(curs, levels)]
        final = levels is steps[0]
        shape = (each, 2 * height, width)
        outs = [(parts, 2 * height, width)] if final else [shape] * colors
        curs = call(functools.partial(join_body, levels, height, final), outs)(sc, *curs, *gots)
        height *= 2
    mine = curs[0]
    return mine, swap_bit(mine, (1, 0))


def local(obj_re, obj_im, probe_re, probe_im, amps, positions):
    rows, cols = obj_re.shape
    modes, width = probe_re.shape[0], probe_re.shape[1]
    rim = width // 2
    n_row, n_col = lax.axis_size("row"), lax.axis_size("col")
    n_dev = n_row * n_col
    sizes = (n_row, n_col, rows, cols, rim)
    right_np, left_np = tables(width)
    right_t, left_t = jnp.asarray(right_np), jnp.asarray(left_np)
    mine = jnp.broadcast_to(jnp.pad(positions.reshape(1, 2), ((0, 0), (0, 126))), (n_dev, 128))
    spots = lax.all_to_all(mine, ("row", "col"), 0, 0, tiled=True)[:, :2].reshape(-1)
    here = jnp.stack([lax.axis_index("row"), lax.axis_index("col")]).astype(jnp.int32)
    sc = jnp.concatenate([here, spots])
    view = amps.reshape(width, width)

    grid = (n_row * rows + 2 * rim, n_col * cols + 3 * rim)
    (denom,) = call(
        functools.partial(light_body, sizes, n_dev),
        [(rows, cols)],
        [pltpu.VMEM(grid, F32), pltpu.VMEM((2, width, width + rim), F32)],
    )(sc, probe_re, probe_im)

    strip = (2, width, cols)
    tile = (2, rows, cols)
    tall = pltpu.VMEM((2, rows + 2 * rim, cols), F32)
    halo = call(functools.partial(halo_body, sizes), [strip] * 3, [tall])
    fold = call(functools.partial(fold_body, sizes), [tile] * 3, [tall])
    step = call(functools.partial(step_body, sizes), [tile])
    scratch = [pltpu.VMEM((modes, 2 * width, width), F32), pltpu.VMEM((2, width, width), F32)]
    terms = (2 * modes + 1, rim, width)

    state = jnp.stack([obj_re, obj_im])
    for turn in range(ITERS):
        last = turn == ITERS - 1
        far, near = swap_far(state, "row"), swap_near(state, "row")
        mid, to_near, to_far = halo(sc, state, near, far)
        far, near = swap_far(to_far, "col"), swap_near(to_near, "col")
        outs = [strip] * 3 + ([terms] * 2 if last else [])
        scr = scratch + ([pltpu.VMEM((2 * modes + 1, width, width), F32)] if last else [])
        res = call(functools.partial(view_body, sizes, last), outs, scr)(
            sc, mid, near, far, probe_re, probe_im, view, right_t, left_t
        )
        gm, to_near, to_far = res[:3]
        far, near = swap_far(to_far, "col"), swap_near(to_near, "col")
        own, to_near, to_far = fold(sc, gm, near, far)
        far, near = swap_far(to_far, "row"), swap_near(to_near, "row")
        (state,) = step(sc, state, own, near, far, denom)
    mine, other = sum_terms(sc, res[3], res[4], n_row, n_col)
    shape = (modes, width, width)
    new_re, new_im = call(functools.partial(probe_body, rim), [shape] * 2)(
        sc, mine, other, probe_re, probe_im
    )
    return (state[0], state[1], new_re, new_im)


def solution(mesh):
    placed = (
        P("row", "col"),
        P("row", "col"),
        P(),
        P(),
        P("row", "col", None, None, None),
        P("row", "col", None, None),
    )
    return jax.shard_map(
        local,
        mesh=mesh,
        in_specs=placed,
        out_specs=(P("row", "col"), P("row", "col"), P(), P()),
        check_vma=False,
    )
```

```python
import functools
import math

import jax
import jax.numpy as jnp
import numpy as np
from jax import lax
from jax.experimental import pallas as pl
from jax.experimental.pallas import tpu as pltpu
from jax.sharding import PartitionSpec as P


ITERS = 3

amp_floor = 0.25
light_ratio = 0.1
mass_ratio = 0.1
probe_step = 6.0

F32 = jnp.float32
BF16 = jnp.bfloat16
HEAD = 2


def tables(width):
    index = np.arange(width)
    angle = (index[:, None] * index[None, :] % width) * (2.0 * math.pi / width)
    real = (np.cos(angle) / math.sqrt(width)).astype(np.float32)
    imag = (-np.sin(angle) / math.sqrt(width)).astype(np.float32)
    right = np.block([[real, imag], [-imag, real]]).astype(BF16)
    left = np.block([[real, -imag], [imag, real]]).astype(BF16)
    return right, left


def near_pairs(count):
    return [(i, i ^ 1) for i in range(count)]


def far_pairs(count):
    return [(i, (i + 1 if i % 2 else i - 1) % count) for i in range(count)]


def swap(array, axis, far):
    pairs = (far_pairs if far else near_pairs)(lax.axis_size(axis))
    return lax.ppermute(array, axis, pairs)


def swap_both(to_near, to_far, axis):
    return swap(to_near, axis, False), swap(to_far, axis, True)


def call(body, outs, scratch=(), smem=1, extra=1 << 20, cost=None):
    def run(*args):
        held = sum(4 * math.prod(s) for s in outs) + sum(a.size * a.dtype.itemsize for a in args[smem:])
        held += sum(math.prod(s.shape) * 4 for s in scratch)
        grant = held + extra
        specs = [pl.BlockSpec(memory_space=pltpu.SMEM)] * smem
        specs += [pl.BlockSpec(memory_space=pltpu.VMEM)] * (len(args) - smem)
        return pl.pallas_call(
            body,
            out_shape=[jax.ShapeDtypeStruct(s, F32) for s in outs],
            in_specs=specs,
            out_specs=[pl.BlockSpec(memory_space=pltpu.VMEM)] * len(outs),
            scratch_shapes=list(scratch),
            compiler_params=pltpu.CompilerParams(vmem_limit_bytes=grant),
            cost_estimate=cost,
        )(*args)

    return run


class Place:
    def __init__(self, sc, sizes):
        n_row, n_col, rows, cols, rim = sizes
        self.i, self.j = sc[0], sc[1]
        self.even_row = self.i % 2 == 0
        self.even_col = self.j % 2 == 0
        self.up = self.i > 0
        self.down = self.i < n_row - 1
        self.has_left = self.j > 0
        self.has_right = self.j < n_col - 1
        self.far_row = jnp.where(self.even_row, self.i, n_row - 1 - self.i) > 0
        self.far_col = jnp.where(self.even_col, self.j, n_col - 1 - self.j) > 0
        near = jnp.where(self.even_col, self.j + 1, self.j - 1)
        far = jnp.where(self.even_col, self.j - 1, self.j + 1)
        far = jnp.where(self.far_col, far, self.j)

        def row_of(col):
            at = sc[HEAD + 2 * (self.i * n_col + col)]
            return pl.multiple_of(at - (self.i * rows - rim), rim // 2)

        self.row = row_of(self.j)
        self.near_row = row_of(near)
        self.far_row_at = row_of(far)
        self.col = sc[HEAD + 2 * (self.i * n_col + self.j) + 1] - (self.j * cols - rim)


def light_body(sizes, n_dev, sc, pr, pi, out, buf, pw):
    n_row, n_col, rows, cols, rim = sizes
    width = 2 * rim
    half = rim // 2
    power = jnp.sum(pr[...] * pr[...] + pi[...] * pi[...], axis=0)
    lane = lax.broadcasted_iota(jnp.int32, (width, rim), 1)
    a, b = power[:, :rim], power[:, rim:]
    ra, rb = pltpu.roll(a, half, 1), pltpu.roll(b, half, 1)
    zero = jnp.zeros((width, rim), F32)
    pw[0] = jnp.concatenate([a, b, zero], axis=1)
    pw[1] = jnp.concatenate(
        [jnp.where(lane < half, 0.0, ra), jnp.where(lane < half, ra, rb), jnp.where(lane < half, rb, 0.0)],
        axis=1,
    )
    buf[...] = jnp.zeros_like(buf)

    def add(p, carry):
        row = pl.multiple_of(sc[HEAD + 2 * p] + rim, half)
        col = sc[HEAD + 2 * p + 1] + rim
        odd = (col // half) % 2
        at = (pl.ds(row, width), pl.ds(pl.multiple_of(col - odd * half, rim), width + rim))
        buf[at] += pw[odd]
        return carry

    lax.fori_loop(0, n_dev, add, 0)

    def peak_of(k, best):
        at = pl.multiple_of(k * rows + rim, rim)
        return jnp.maximum(best, jnp.max(buf[pl.ds(at, rows), rim : rim + n_col * cols]))

    peak = lax.fori_loop(0, n_row, peak_of, jnp.float32(0.0))
    mine = buf[
        pl.ds(pl.multiple_of(sc[0] * rows + rim, rim), rows),
        pl.ds(pl.multiple_of(sc[1] * cols + rim, rim), cols),
    ]
    out[...] = mine + light_ratio * peak


def stage_body(*refs):
    count = len(refs) // 2
    ins, outs, sem = refs[:count], refs[count : 2 * count], refs[2 * count]
    copies = [pltpu.make_async_copy(a, b, sem.at[k]) for k, (a, b) in enumerate(zip(ins, outs))]
    for copy in copies:
        copy.start()
    for copy in copies:
        copy.wait()


def stage(*arrays):
    size = sum(a.size * a.dtype.itemsize for a in arrays)
    return pl.pallas_call(
        stage_body,
        out_shape=[jax.ShapeDtypeStruct(a.shape, a.dtype) for a in arrays],
        in_specs=[pl.BlockSpec(memory_space=pl.ANY)] * len(arrays),
        out_specs=[pl.BlockSpec(memory_space=pltpu.VMEM)] * len(arrays),
        scratch_shapes=[pltpu.SemaphoreType.DMA((len(arrays),))],
        compiler_params=pltpu.CompilerParams(vmem_limit_bytes=size + (1 << 20)),
        cost_estimate=pl.CostEstimate(flops=0, bytes_accessed=2 * size, transcendentals=0),
    )(*arrays)


def halo_body(sizes, sc, s, near, far, mid, to_near, to_far, ext):
    _, _, rows, _, rim = sizes
    at = Place(sc, sizes)
    width = 2 * rim
    above = jnp.where(at.even_row, far[...], near[...])
    below = jnp.where(at.even_row, near[...], far[...])
    ext[:, :rim] = jnp.where(at.up, above, 0.0)
    ext[:, rim : rim + rows] = s[...]
    ext[:, rim + rows :] = jnp.where(at.down, below, 0.0)
    mid[...] = ext[:, pl.ds(at.row, width)]
    to_near[...] = ext[:, pl.ds(at.near_row, width)]
    to_far[...] = ext[:, pl.ds(at.far_row_at, width)]


def view_body(sizes, last, sc, mid, near, far, pr, pi, view, right_t, left_t, *refs):
    if last:
        gm, to_near, to_far, keep, send, spec_scr, win_scr, term_scr = refs
    else:
        gm, to_near, to_far, spec_scr, win_scr = refs
    _, _, _, _, rim = sizes
    at = Place(sc, sizes)
    modes, width = pr.shape[0], pr.shape[1]
    half = rim // 2
    lane = lax.broadcasted_iota(jnp.int32, (width, rim), 1)
    first = at.col == 0
    middle = at.col == half
    for part in range(2):
        a, b = near[part], far[part]
        lft = jnp.where(at.has_left, jnp.where(at.even_col, b, a), 0.0)
        rgt = jnp.where(at.has_right, jnp.where(at.even_col, a, b), 0.0)
        own = mid[part]
        rl, ro, rr = (pltpu.roll(t, half, 1) for t in (lft, own, rgt))
        win_scr[part, :, :rim] = jnp.where(
            first, lft, jnp.where(middle, jnp.where(lane < half, rl, ro), own)
        )
        win_scr[part, :, rim:] = jnp.where(
            first, own, jnp.where(middle, jnp.where(lane < half, ro, rr), rgt)
        )
    total = jnp.zeros((width, width), F32)
    for m in range(modes):
        wr, wi = win_scr[0], win_scr[1]
        psi = jnp.concatenate(
            [pr[m] * wr - pi[m] * wi, pr[m] * wi + pi[m] * wr], axis=1
        ).astype(BF16)
        mixed = jnp.dot(psi, right_t[...], preferred_element_type=F32).astype(BF16)
        tall = jnp.concatenate([mixed[:, :width], mixed[:, width:]], axis=0)
        spec = jnp.dot(left_t[...], tall, preferred_element_type=F32)
        spec_scr[m] = spec
        total = total + (spec[:width] * spec[:width] + spec[width:] * spec[width:])
    factor = view[...] / jnp.maximum(jnp.sqrt(total), amp_floor) - 1.0
    grad = [jnp.zeros((width, width), F32), jnp.zeros((width, width), F32)]
    for m in range(modes):
        change = jnp.concatenate(
            [spec_scr[m, :width] * factor, spec_scr[m, width:] * factor], axis=1
        ).astype(BF16)
        mixed = jnp.dot(change, left_t[...], preferred_element_type=F32).astype(BF16)
        tall = jnp.concatenate([mixed[:, :width], mixed[:, width:]], axis=0)
        back = jnp.dot(right_t[...], tall, preferred_element_type=F32)
        er, ei = back[:width], back[width:]
        grad[0] = grad[0] + (pr[m] * er + pi[m] * ei)
        grad[1] = grad[1] + (pr[m] * ei - pi[m] * er)
        if last:
            wr, wi = win_scr[0], win_scr[1]
            term_scr[m] = wr * er + wi * ei
            term_scr[modes + m] = wr * ei - wi * er
    for part in range(2):
        a, b = grad[part][:, :rim], grad[part][:, rim:]
        ra, rb = pltpu.roll(a, half, 1), pltpu.roll(b, half, 1)
        low = lane < half
        lft = jnp.where(first, a, jnp.where(middle, jnp.where(low, 0.0, ra), 0.0))
        own = jnp.where(first, b, jnp.where(middle, jnp.where(low, ra, rb), a))
        rgt = jnp.where(first, 0.0, jnp.where(middle, jnp.where(low, rb, 0.0), b))
        gm[part] = own
        to_near[part] = jnp.where(at.even_col, rgt, lft)
        to_far[part] = jnp.where(at.even_col, lft, rgt)
    if last:
        wr, wi = win_scr[0], win_scr[1]
        term_scr[2 * modes] = wr * wr + wi * wi
        bit = at.j % 2
        keep[...] = term_scr[:, pl.ds(pl.multiple_of(bit * rim, rim), rim)]
        send[...] = term_scr[:, pl.ds(pl.multiple_of((1 - bit) * rim, rim), rim)]


def fold_body(sizes, sc, gm, near, far, own, to_near, to_far, buf):
    _, _, rows, _, rim = sizes
    at = Place(sc, sizes)
    width = 2 * rim
    buf[...] = jnp.zeros_like(buf)
    buf[:, pl.ds(at.row, width)] = gm[...]
    buf[:, pl.ds(at.near_row, width)] += near[...]
    buf[:, pl.ds(at.far_row_at, width)] += jnp.where(at.far_col, far[...], 0.0)
    top, bottom = buf[:, :rim], buf[:, rim + rows :]
    own[...] = buf[:, rim : rim + rows]
    to_near[...] = jnp.where(at.even_row, bottom, top)
    to_far[...] = jnp.where(at.even_row, top, bottom)


def step_body(sizes, sc, s, own, near, far, denom, out):
    at = Place(sc, sizes)
    grad = own[...] + near[...] + jnp.where(at.far_row, far[...], 0.0)
    out[...] = s[...] + grad / denom[...][None]


def bit_of(sc, axis, level):
    return lax.shift_right_logical(sc[axis], level) % 2


def halve_body(levels, height, shared, sc, *refs):
    count = len(levels)
    ins = 1 if shared else count
    cur, got, out = refs[:ins], refs[ins : 2 * ins], refs[2 * ins :]
    for c, (axis, level) in enumerate(levels):
        bit = bit_of(sc, axis, level)
        each = out[2 * c].shape[0]
        for which, offset in ((0, bit * height), (1, (1 - bit) * height)):
            rows = pl.ds(pl.multiple_of(offset, 8), height)
            if shared:
                at = (slice(c * each, (c + 1) * each), rows)
                out[2 * c + which][...] = cur[0][at] + got[0][at]
            else:
                out[2 * c + which][...] = cur[c][:, rows] + got[c][:, rows]


def gather_sum_body(count, sc, *refs):
    cur, got, out = refs[:count], refs[count : 2 * count], refs[2 * count]
    each = cur[0].shape[0]
    for c in range(count):
        out[c * each : (c + 1) * each] = cur[c][...] + got[c][...]


def spread_sum_body(count, sc, cur, got, *out):
    each = out[0].shape[0]
    for c in range(count):
        at = slice(c * each, (c + 1) * each)
        out[c][...] = cur[at] + got[at]


def sum_body(sc, cur, got, out):
    out[...] = cur[...] + got[...]


def join_body(levels, height, shared, sc, *refs):
    count = len(levels)
    cur, got, out = refs[:count], refs[count : 2 * count], refs[2 * count :]
    for c, (axis, level) in enumerate(levels):
        bit = bit_of(sc, axis, level)
        each = cur[c].shape[0]
        for src, offset in ((cur[c], bit * height), (got[c], (1 - bit) * height)):
            rows = pl.ds(pl.multiple_of(offset, 8), height)
            if shared:
                out[0][c * each : (c + 1) * each, rows] = src[...]
            else:
                out[c][:, rows] = src[...]


def probe_body(rim, sc, mine, got, pr, pi, new_re, new_im):
    modes = pr.shape[0]
    pixels = 4 * rim * rim
    bit = sc[1] % 2
    mean = (jnp.sum(mine[2 * modes]) + jnp.sum(got[2 * modes])) / pixels
    for src, offset in ((mine, bit * rim), (got, (1 - bit) * rim)):
        rows = pl.ds(pl.multiple_of(offset, rim), rim)
        scale = probe_step / (src[2 * modes] + mass_ratio * mean)
        for m in range(modes):
            new_re[m, rows] = pr[m, rows] + src[m] * scale
            new_im[m, rows] = pi[m, rows] + src[modes + m] * scale


def swap_bit(array, where):
    axis, level = where
    name = ("row", "col")[axis]
    count = lax.axis_size(name)
    return lax.ppermute(array, name, [(i, i ^ (1 << level)) for i in range(count)])


def sum_terms(sc, keep, send, n_row, n_col, beside):
    parts, height, width = keep.shape
    colors = 3
    each = parts // colors
    row_bits = [(0, k) for k in range(n_row.bit_length() - 1)]
    col_bits = [(1, k) for k in range(1, n_col.bit_length() - 1)]
    rest = []
    while row_bits or col_bits:
        if row_bits:
            rest.append(row_bits.pop(0))
        if col_bits:
            rest.append(col_bits.pop(0))
    turn = rest[:colors]
    orders = [turn[c:] + turn[:c] for c in range(colors)]
    tail = rest[colors:]
    got = swap_bit(send, (1, 0))
    curs, gots, shared = [keep], [got], True
    steps = []
    for r in range(len(turn)):
        levels = [orders[c][r] for c in range(colors)]
        height //= 2
        outs = [(each, height, width)] * (2 * colors)
        res = call(functools.partial(halve_body, levels, height, shared), outs)(sc, *curs, *gots)
        curs, sends = res[0::2], res[1::2]
        gots = [swap_bit(a, w) for a, w in zip(sends, levels)]
        gots = beside(r, gots)
        shared = False
        steps.append(levels)
    (cur,) = call(functools.partial(gather_sum_body, colors), [(parts, height, width)])(
        sc, *curs, *gots
    )
    for where in tail[:-1]:
        got = swap_bit(cur, where)
        (cur,) = call(sum_body, [cur.shape])(sc, cur, got)
    got = swap_bit(cur, tail[-1])
    curs = call(functools.partial(spread_sum_body, colors), [(each, height, width)] * colors)(
        sc, cur, got
    )
    for levels in reversed(steps):
        gots = [swap_bit(a, w) for a, w in zip(curs, levels)]
        final = levels is steps[0]
        shape = (each, 2 * height, width)
        outs = [(parts, 2 * height, width)] if final else [shape] * colors
        curs = call(functools.partial(join_body, levels, height, final), outs)(sc, *curs, *gots)
        height *= 2
    mine = curs[0]
    return mine, swap_bit(mine, (1, 0))


def local(obj_re, obj_im, probe_re, probe_im, amps, positions):
    rows, cols = obj_re.shape
    modes, width = probe_re.shape[0], probe_re.shape[1]
    rim = width // 2
    n_row, n_col = lax.axis_size("row"), lax.axis_size("col")
    n_dev = n_row * n_col
    sizes = (n_row, n_col, rows, cols, rim)
    right_np, left_np = tables(width)
    right_t, left_t = jnp.asarray(right_np), jnp.asarray(left_np)
    mine = jnp.broadcast_to(jnp.pad(positions.reshape(1, 2), ((0, 0), (0, 126))), (n_dev, 128))
    spots = lax.all_to_all(mine, ("row", "col"), 0, 0, tiled=True)
    spots = spots[:, :2].reshape(-1)
    here = jnp.stack([lax.axis_index("row"), lax.axis_index("col")]).astype(jnp.int32)
    sc = jnp.concatenate([here, spots])
    view = amps.reshape(width, width)
    probe_re, probe_im, view, right_t, left_t = stage(probe_re, probe_im, view, right_t, left_t)

    grid = (n_row * rows + 2 * rim, n_col * cols + 3 * rim)
    (denom,) = call(
        functools.partial(light_body, sizes, n_dev),
        [(rows, cols)],
        [pltpu.VMEM(grid, F32), pltpu.VMEM((2, width, width + rim), F32)],
        extra=4 << 20,
        cost=pl.CostEstimate(flops=8 * n_dev * width * width, bytes_accessed=10**7, transcendentals=0),
    )(sc, probe_re, probe_im)

    strip = (2, width, cols)
    tile = (2, rows, cols)
    tall = pltpu.VMEM((2, rows + 2 * rim, cols), F32)
    halo = call(functools.partial(halo_body, sizes), [strip] * 3, [tall])
    fold = call(functools.partial(fold_body, sizes), [tile] * 3, [tall])
    step = call(functools.partial(step_body, sizes), [tile])
    scratch = [pltpu.VMEM((modes, 2 * width, width), F32), pltpu.VMEM((2, width, width), F32)]
    terms = (2 * modes + 1, rim, width)

    state = jnp.stack([obj_re, obj_im])
    for turn in range(ITERS):
        last = turn == ITERS - 1
        near, far = swap_both(state, state, "row")
        mid, to_near, to_far = halo(sc, state, near, far)
        near, far = swap_both(to_near, to_far, "col")
        outs = [strip] * 3 + ([terms] * 2 if last else [])
        scr = scratch + ([pltpu.VMEM((2 * modes + 1, width, width), F32)] if last else [])
        res = call(functools.partial(view_body, sizes, last), outs, scr, extra=8 << 20)(
            sc, mid, near, far, probe_re, probe_im, view, right_t, left_t
        )
        gm, to_near, to_far = res[:3]
        near, far = swap_both(to_near, to_far, "col")
        if last:
            break
        own, to_near, to_far = fold(sc, gm, near, far)
        near, far = swap_both(to_near, to_far, "row")
        (state,) = step(sc, state, own, near, far, denom)

    held = {}

    def beside(r, gots):
        if r == 0:
            *gots, a, b = lax.optimization_barrier([*gots, near, far])
            held["own"], to_near, to_far = fold(sc, gm, a, b)
            held["both"] = swap_both(to_near, to_far, "row")
        elif r == 1:
            *gots, a, b = lax.optimization_barrier([*gots, *held["both"]])
            (held["state"],) = step(sc, state, held["own"], a, b, denom)
        return gots

    mine, other = sum_terms(sc, res[3], res[4], n_row, n_col, beside)
    shape = (modes, width, width)
    new_re, new_im = call(functools.partial(probe_body, rim), [shape] * 2)(
        sc, mine, other, probe_re, probe_im
    )
    return (held["state"][0], held["state"][1], new_re, new_im)


def solution(mesh):
    placed = (
        P("row", "col"),
        P("row", "col"),
        P(),
        P(),
        P("row", "col", None, None, None),
        P("row", "col", None, None),
    )

    return jax.shard_map(
        local,
        mesh=mesh,
        in_specs=placed,
        out_specs=(P("row", "col"), P("row", "col"), P(), P()),
        check_vma=False,
    )
```

```python
import functools
import math

import jax
import jax.numpy as jnp
import numpy as np
from jax import lax
from jax.experimental import pallas as pl
from jax.experimental.pallas import tpu as pltpu
from jax.sharding import PartitionSpec as P


ITERS = 3

amp_floor = 0.25
light_ratio = 0.1
mass_ratio = 0.1
probe_step = 6.0

F32 = jnp.float32
BF16 = jnp.bfloat16
COLORS = 3


def tables(width):
    index = np.arange(width)
    angle = (index[:, None] * index[None, :] % width) * (2.0 * math.pi / width)
    real = (np.cos(angle) / math.sqrt(width)).astype(np.float32)
    imag = (-np.sin(angle) / math.sqrt(width)).astype(np.float32)
    right = np.block([[real, imag], [-imag, real]]).astype(BF16)
    left = np.block([[real, -imag], [imag, real]]).astype(BF16)
    return right, left


def near_pairs(count):
    return [(i, i ^ 1) for i in range(count)]


def far_pairs(count):
    return [(i, (i + 1 if i % 2 else i - 1) % count) for i in range(count)]


def swap(array, axis, far):
    pairs = (far_pairs if far else near_pairs)(lax.axis_size(axis))
    return lax.ppermute(array, axis, pairs)


def swap_both(to_near, to_far, axis):
    return swap(to_near, axis, False), swap(to_far, axis, True)


def call(body, outs, scratch=(), smem=0, extra=1 << 20, cost=None):
    def run(*args):
        held = sum(4 * math.prod(s) for s in outs) + sum(a.size * a.dtype.itemsize for a in args[smem:])
        held += sum(math.prod(s.shape) * 4 for s in scratch)
        grant = held + extra
        specs = [pl.BlockSpec(memory_space=pltpu.SMEM)] * smem
        specs += [pl.BlockSpec(memory_space=pltpu.VMEM)] * (len(args) - smem)
        return pl.pallas_call(
            body,
            out_shape=[jax.ShapeDtypeStruct(s, F32) for s in outs],
            in_specs=specs,
            out_specs=[pl.BlockSpec(memory_space=pltpu.VMEM)] * len(outs),
            scratch_shapes=list(scratch),
            compiler_params=pltpu.CompilerParams(vmem_limit_bytes=grant),
            cost_estimate=cost,
        )(*args)

    return run


class Place:
    def __init__(self, sc, sizes):
        n_row, n_col, rows, cols, rim = sizes
        self.i, self.j = lax.axis_index("row"), lax.axis_index("col")
        self.even_row = self.i % 2 == 0
        self.even_col = self.j % 2 == 0
        self.up = self.i > 0
        self.down = self.i < n_row - 1
        self.has_left = self.j > 0
        self.has_right = self.j < n_col - 1
        self.far_row = jnp.where(self.even_row, self.i, n_row - 1 - self.i) > 0
        self.far_col = jnp.where(self.even_col, self.j, n_col - 1 - self.j) > 0
        if sc is None:
            return
        near = jnp.where(self.even_col, self.j + 1, self.j - 1)
        far = jnp.where(self.even_col, self.j - 1, self.j + 1)
        far = jnp.where(self.far_col, far, self.j)

        spots = sc[...]
        index = lax.broadcasted_iota(jnp.int32, spots.shape, 0) * spots.shape[1]
        index = index + lax.broadcasted_iota(jnp.int32, spots.shape, 1)

        def known(col, part):
            wanted = 2 * (self.i * n_col + col) + part
            return jnp.sum(jnp.where(index == wanted, spots, 0.0)).astype(jnp.int32)

        def row_of(col):
            return pl.multiple_of(known(col, 0) - (self.i * rows - rim), rim // 2)

        self.row = row_of(self.j)
        self.near_row = row_of(near)
        self.far_row_at = row_of(far)
        self.col = known(self.j, 1) - (self.j * cols - rim)


def light_body(sizes, n_dev, sc, pr, pi, out, buf, pw):
    n_row, n_col, rows, cols, rim = sizes
    width = 2 * rim
    half = rim // 2
    power = jnp.sum(pr[...] * pr[...] + pi[...] * pi[...], axis=0)
    lane = lax.broadcasted_iota(jnp.int32, (width, rim), 1)
    a, b = power[:, :rim], power[:, rim:]
    ra, rb = pltpu.roll(a, half, 1), pltpu.roll(b, half, 1)
    zero = jnp.zeros((width, rim), F32)
    pw[0] = jnp.concatenate([a, b, zero], axis=1)
    pw[1] = jnp.concatenate(
        [jnp.where(lane < half, 0.0, ra), jnp.where(lane < half, ra, rb), jnp.where(lane < half, rb, 0.0)],
        axis=1,
    )
    buf[...] = jnp.zeros_like(buf)

    def add(p, carry):
        row = pl.multiple_of(sc[2 * p] + rim, half)
        col = sc[2 * p + 1] + rim
        odd = (col // half) % 2
        at = (pl.ds(row, width), pl.ds(pl.multiple_of(col - odd * half, rim), width + rim))
        buf[at] += pw[odd]
        return carry

    lax.fori_loop(0, n_dev, add, 0)

    def peak_of(k, best):
        at = pl.multiple_of(k * rows + rim, rim)
        return jnp.maximum(best, jnp.max(buf[pl.ds(at, rows), rim : rim + n_col * cols]))

    peak = lax.fori_loop(0, n_row, peak_of, jnp.float32(0.0))
    mine = buf[
        pl.ds(pl.multiple_of(lax.axis_index("row") * rows + rim, rim), rows),
        pl.ds(pl.multiple_of(lax.axis_index("col") * cols + rim, rim), cols),
    ]
    out[...] = mine + light_ratio * peak


def stage_body(*refs):
    count = len(refs) // 2
    ins, outs, sem = refs[:count], refs[count : 2 * count], refs[2 * count]
    copies = [pltpu.make_async_copy(a, b, sem.at[k]) for k, (a, b) in enumerate(zip(ins, outs))]
    for copy in copies:
        copy.start()
    for copy in copies:
        copy.wait()


def stage(*arrays):
    size = sum(a.size * a.dtype.itemsize for a in arrays)
    return pl.pallas_call(
        stage_body,
        out_shape=[jax.ShapeDtypeStruct(a.shape, a.dtype) for a in arrays],
        in_specs=[pl.BlockSpec(memory_space=pltpu.HBM)] * len(arrays),
        out_specs=[pl.BlockSpec(memory_space=pltpu.VMEM)] * len(arrays),
        scratch_shapes=[pltpu.SemaphoreType.DMA((len(arrays),))],
        compiler_params=pltpu.CompilerParams(vmem_limit_bytes=size + (1 << 20)),
        cost_estimate=pl.CostEstimate(flops=0, bytes_accessed=2 * size, transcendentals=0),
    )(*arrays)


def halo_body(sizes, sc, s, near, far, mid, to_near, to_far, ext):
    _, _, rows, _, rim = sizes
    at = Place(sc, sizes)
    width = 2 * rim
    above = jnp.where(at.even_row, far[...], near[...])
    below = jnp.where(at.even_row, near[...], far[...])
    ext[:, :rim] = jnp.where(at.up, above, 0.0)
    ext[:, rim : rim + rows] = s[...]
    ext[:, rim + rows :] = jnp.where(at.down, below, 0.0)
    mid[...] = ext[:, pl.ds(at.row, width)]
    to_near[...] = ext[:, pl.ds(at.near_row, width)]
    to_far[...] = ext[:, pl.ds(at.far_row_at, width)]


def view_body(sizes, last, sc, mid, near, far, pr, pi, view, right_t, left_t, *refs):
    if last:
        gm, to_near, to_far, *parts, spec_scr, win_scr, term_scr = refs
    else:
        gm, to_near, to_far, spec_scr, win_scr = refs
    _, _, _, _, rim = sizes
    at = Place(sc, sizes)
    modes, width = pr.shape[0], pr.shape[1]
    half = rim // 2
    lane = lax.broadcasted_iota(jnp.int32, (width, rim), 1)
    first = at.col == 0
    middle = at.col == half
    for part in range(2):
        a, b = near[part], far[part]
        lft = jnp.where(at.has_left, jnp.where(at.even_col, b, a), 0.0)
        rgt = jnp.where(at.has_right, jnp.where(at.even_col, a, b), 0.0)
        own = mid[part]
        rl, ro, rr = (pltpu.roll(t, half, 1) for t in (lft, own, rgt))
        win_scr[part, :, :rim] = jnp.where(
            first, lft, jnp.where(middle, jnp.where(lane < half, rl, ro), own)
        )
        win_scr[part, :, rim:] = jnp.where(
            first, own, jnp.where(middle, jnp.where(lane < half, ro, rr), rgt)
        )
    total = jnp.zeros((width, width), F32)
    for m in range(modes):
        wr, wi = win_scr[0], win_scr[1]
        psi = jnp.concatenate(
            [pr[m] * wr - pi[m] * wi, pr[m] * wi + pi[m] * wr], axis=1
        ).astype(BF16)
        mixed = jnp.dot(psi, right_t[...], preferred_element_type=F32).astype(BF16)
        tall = jnp.concatenate([mixed[:, :width], mixed[:, width:]], axis=0)
        spec = jnp.dot(left_t[...], tall, preferred_element_type=F32)
        spec_scr[m] = spec
        total = total + (spec[:width] * spec[:width] + spec[width:] * spec[width:])
    factor = view[...] / jnp.maximum(jnp.sqrt(total), amp_floor) - 1.0
    grad = [jnp.zeros((width, width), F32), jnp.zeros((width, width), F32)]
    for m in range(modes):
        change = jnp.concatenate(
            [spec_scr[m, :width] * factor, spec_scr[m, width:] * factor], axis=1
        ).astype(BF16)
        mixed = jnp.dot(change, left_t[...], preferred_element_type=F32).astype(BF16)
        tall = jnp.concatenate([mixed[:, :width], mixed[:, width:]], axis=0)
        back = jnp.dot(right_t[...], tall, preferred_element_type=F32)
        er, ei = back[:width], back[width:]
        grad[0] = grad[0] + (pr[m] * er + pi[m] * ei)
        grad[1] = grad[1] + (pr[m] * ei - pi[m] * er)
        if last:
            wr, wi = win_scr[0], win_scr[1]
            term_scr[m] = wr * er + wi * ei
            term_scr[modes + m] = wr * ei - wi * er
    for part in range(2):
        a, b = grad[part][:, :rim], grad[part][:, rim:]
        ra, rb = pltpu.roll(a, half, 1), pltpu.roll(b, half, 1)
        low = lane < half
        lft = jnp.where(first, a, jnp.where(middle, jnp.where(low, 0.0, ra), 0.0))
        own = jnp.where(first, b, jnp.where(middle, jnp.where(low, ra, rb), a))
        rgt = jnp.where(first, 0.0, jnp.where(middle, jnp.where(low, rb, 0.0), b))
        gm[part] = own
        to_near[part] = jnp.where(at.even_col, rgt, lft)
        to_far[part] = jnp.where(at.even_col, lft, rgt)
    if last:
        wr, wi = win_scr[0], win_scr[1]
        term_scr[2 * modes] = wr * wr + wi * wi
        bit = at.j % 2
        each = parts[0].shape[0]
        for k, part in enumerate(parts):
            at = slice((k // 2) * each, (k // 2 + 1) * each)
            offset = (1 - bit if k % 2 else bit) * rim
            part[...] = term_scr[at, pl.ds(pl.multiple_of(offset, rim), rim)]


def fold_body(sizes, sc, gm, near, far, own, to_near, to_far, buf):
    _, _, rows, _, rim = sizes
    at = Place(sc, sizes)
    width = 2 * rim
    buf[...] = jnp.zeros_like(buf)
    buf[:, pl.ds(at.row, width)] = gm[...]
    buf[:, pl.ds(at.near_row, width)] += near[...]
    buf[:, pl.ds(at.far_row_at, width)] += jnp.where(at.far_col, far[...], 0.0)
    top, bottom = buf[:, :rim], buf[:, rim + rows :]
    own[...] = buf[:, rim : rim + rows]
    to_near[...] = jnp.where(at.even_row, bottom, top)
    to_far[...] = jnp.where(at.even_row, top, bottom)


def step_body(sizes, s, own, near, far, denom, out):
    at = Place(None, sizes)
    grad = own[...] + near[...] + jnp.where(at.far_row, far[...], 0.0)
    out[...] = s[...] + grad / denom[...][None]


def bit_of(axis, level):
    return lax.shift_right_logical(lax.axis_index(("row", "col")[axis]), level) % 2


def halve_body(where, cur, got, keep, send):
    bit = bit_of(*where)
    height = keep.shape[1]
    for out, offset in ((keep, bit * height), (send, (1 - bit) * height)):
        rows = pl.ds(pl.multiple_of(offset, 8), height)
        out[...] = cur[:, rows] + got[:, rows]


def sum_body(cur, got, out):
    out[...] = cur[...] + got[...]


def join_body(where, cur, got, out):
    bit = bit_of(*where)
    height = cur.shape[1]
    for src, offset in ((cur, bit * height), (got, (1 - bit) * height)):
        out[:, pl.ds(pl.multiple_of(offset, 8), height)] = src[...]


def probe_body(rim, *refs):
    colors = (len(refs) - 4) // 2
    mine, got = refs[:colors], refs[colors : 2 * colors]
    pr, pi, new_re, new_im = refs[2 * colors :]
    modes = pr.shape[0]
    each = mine[0].shape[0]
    pixels = 4 * rim * rim
    bit = lax.axis_index("col") % 2

    def term(src, k):
        return src[k // each][k % each]

    mean = (jnp.sum(term(mine, 2 * modes)) + jnp.sum(term(got, 2 * modes))) / pixels
    for src, offset in ((mine, bit * rim), (got, (1 - bit) * rim)):
        rows = pl.ds(pl.multiple_of(offset, rim), rim)
        scale = probe_step / (term(src, 2 * modes) + mass_ratio * mean)
        for m in range(modes):
            new_re[m, rows] = pr[m, rows] + term(src, m) * scale
            new_im[m, rows] = pi[m, rows] + term(src, modes + m) * scale


def swap_bit(array, where):
    axis, level = where
    name = ("row", "col")[axis]
    count = lax.axis_size(name)
    return lax.ppermute(array, name, [(i, i ^ (1 << level)) for i in range(count)])


def sum_terms(keeps, sends, n_row, n_col, beside):
    colors = len(keeps)
    each, height, width = keeps[0].shape
    row_bits = [(0, k) for k in range(n_row.bit_length() - 1)]
    col_bits = [(1, k) for k in range(1, n_col.bit_length() - 1)]
    rest = []
    while row_bits or col_bits:
        if row_bits:
            rest.append(row_bits.pop(0))
        if col_bits:
            rest.append(col_bits.pop(0))
    turn = rest[:colors]
    orders = [turn[c:] + turn[:c] for c in range(colors)]
    tail = rest[colors:]
    curs = list(keeps)
    gots = [swap_bit(a, (1, 0)) for a in sends]
    for r in range(len(turn)):
        height //= 2
        for c in range(colors):
            where = orders[c][r]
            outs = [(each, height, width)] * 2
            keep, send = call(functools.partial(halve_body, where), outs)(curs[c], gots[c])
            curs[c], gots[c] = keep, swap_bit(send, where)
        gots = list(beside(r, gots))
    for k, where in enumerate([None] + tail):
        for c in range(colors):
            (curs[c],) = call(sum_body, [curs[c].shape])(curs[c], gots[c])
            if k < len(tail):
                gots[c] = swap_bit(curs[c], tail[k])
    for r in reversed(range(len(turn))):
        for c in range(colors):
            where = orders[c][r]
            got = swap_bit(curs[c], where)
            outs = [(each, 2 * height, width)]
            (curs[c],) = call(functools.partial(join_body, where), outs)(curs[c], got)
        height *= 2
    return curs, [swap_bit(a, (1, 0)) for a in curs]


def enter_body(n_col, pos, spots):
    at = lax.broadcasted_iota(jnp.int32, spots.shape, 0) * spots.shape[1]
    at = at + lax.broadcasted_iota(jnp.int32, spots.shape, 1)
    me = lax.axis_index("row") * n_col + lax.axis_index("col")
    mine = jnp.where(at == 2 * me, pos[0], jnp.where(at == 2 * me + 1, pos[1], 0))
    spots[...] = mine.astype(F32)


def all_spots(known, n_row, n_col):
    bits = [(1, k) for k in range(n_col.bit_length() - 1)]
    local_bits = len(bits)
    bits += [(0, k) for k in range(n_row.bit_length() - 1)]
    stops = []
    for where in bits:
        known = known + swap_bit(known, where)
        stops.append(known)
    return stops[local_bits - 1], known


def local(obj_re, obj_im, probe_re, probe_im, amps, positions):
    rows, cols = obj_re.shape
    modes, width = probe_re.shape[0], probe_re.shape[1]
    rim = width // 2
    n_row, n_col = lax.axis_size("row"), lax.axis_size("col")
    n_dev = n_row * n_col
    sizes = (n_row, n_col, rows, cols, rim)
    right_np, left_np = tables(width)
    right_t, left_t = jnp.asarray(right_np), jnp.asarray(left_np)
    state = jnp.stack([obj_re, obj_im])
    shape = (-(-2 * n_row * n_col // 128), 128)
    (known,) = call(functools.partial(enter_body, n_col), [shape], smem=1)(positions.reshape(2))
    sc, every = all_spots(known, n_row, n_col)
    view = amps.reshape(width, width)
    staged = stage(probe_re, probe_im, view, right_t, left_t)
    probe_re, probe_im, view, right_t, left_t = staged

    grid = (n_row * rows + 2 * rim, n_col * cols + 3 * rim)
    (denom,) = call(
        functools.partial(light_body, sizes, n_dev),
        [(rows, cols)],
        [pltpu.VMEM(grid, F32), pltpu.VMEM((2, width, width + rim), F32)],
        1,
        extra=4 << 20,
        cost=pl.CostEstimate(flops=8 * n_dev * width * width, bytes_accessed=10**7, transcendentals=0),
    )(every.reshape(-1).astype(jnp.int32), probe_re, probe_im)

    strip = (2, width, cols)
    tile = (2, rows, cols)
    tall = pltpu.VMEM((2, rows + 2 * rim, cols), F32)
    halo = call(functools.partial(halo_body, sizes), [strip] * 3, [tall])
    fold = call(functools.partial(fold_body, sizes), [tile] * 3, [tall])
    step = call(functools.partial(step_body, sizes), [tile])
    scratch = [pltpu.VMEM((modes, 2 * width, width), F32), pltpu.VMEM((2, width, width), F32)]
    terms = ((2 * modes + 1) // COLORS, rim, width)

    for turn in range(ITERS):
        last = turn == ITERS - 1
        near, far = swap_both(state, state, "row")
        mid, to_near, to_far = halo(sc, state, near, far)
        near, far = swap_both(to_near, to_far, "col")
        outs = [strip] * 3 + ([terms] * 2 * COLORS if last else [])
        scr = scratch + ([pltpu.VMEM((2 * modes + 1, width, width), F32)] if last else [])
        res = call(functools.partial(view_body, sizes, last), outs, scr, extra=8 << 20)(
            sc, mid, near, far, probe_re, probe_im, view, right_t, left_t
        )
        gm, to_near, to_far = res[:3]
        near, far = swap_both(to_near, to_far, "col")
        if last:
            break
        own, to_near, to_far = fold(sc, gm, near, far)
        near, far = swap_both(to_near, to_far, "row")
        (state,) = step(state, own, near, far, denom)

    held = {}

    def beside(r, gots):
        if r == 0:
            gots[0], a, b = lax.optimization_barrier((gots[0], near, far))
            held["own"], to_near, to_far = fold(sc, gm, a, b)
            held["both"] = swap_both(to_near, to_far, "row")
        elif r == 1:
            gots[2], a, b = lax.optimization_barrier((gots[2], *held["both"]))
            (held["state"],) = step(state, held["own"], a, b, denom)
        return gots

    mine, other = sum_terms(res[3::2], res[4::2], n_row, n_col, beside)
    shape = (modes, width, width)
    new_re, new_im = call(functools.partial(probe_body, rim), [shape] * 2)(
        *mine, *other, probe_re, probe_im
    )
    return (held["state"][0], held["state"][1], new_re, new_im)


def solution(mesh):
    placed = (
        P("row", "col"),
        P("row", "col"),
        P(),
        P(),
        P("row", "col", None, None, None),
        P("row", "col", None, None),
    )

    return jax.shard_map(
        local,
        mesh=mesh,
        in_specs=placed,
        out_specs=(P("row", "col"), P("row", "col"), P(), P()),
        check_vma=False,
    )
```

```python
import functools
import math

import jax
import jax.numpy as jnp
import numpy as np
from jax import lax
from jax.experimental import pallas as pl
from jax.experimental.pallas import tpu as pltpu
from jax.sharding import PartitionSpec as P


ITERS = 3

amp_floor = 0.25
light_ratio = 0.1
mass_ratio = 0.1
probe_step = 6.0

F32 = jnp.float32
BF16 = jnp.bfloat16
COLORS = 3


def tables(width):
    index = np.arange(width)
    angle = (index[:, None] * index[None, :] % width) * (2.0 * math.pi / width)
    real = (np.cos(angle) / math.sqrt(width)).astype(np.float32)
    imag = (-np.sin(angle) / math.sqrt(width)).astype(np.float32)
    right = np.block([[real, imag], [-imag, real]]).astype(BF16)
    left = np.block([[real, -imag], [imag, real]]).astype(BF16)
    return right, left


def swap_pairs(n_row, n_col, axis, far):
    pairs = []
    for i in range(n_row):
        for j in range(n_col):
            k, count = (i, n_row) if axis == "row" else (j, n_col)
            other = k ^ 1 if not far else (k + 1 if k % 2 else k - 1)
            if axis == "row":
                to = (other, j) if 0 <= other < count else (i, j ^ 1)
            else:
                to = (i, other) if 0 <= other < count else (i ^ 1, j)
            pairs.append((i * n_col + j, to[0] * n_col + to[1]))
    return pairs


def swap(array, axis, far):
    pairs = swap_pairs(lax.axis_size("row"), lax.axis_size("col"), axis, far)
    return lax.ppermute(array, ("row", "col"), pairs)


def swap_both(to_near, to_far, axis):
    return swap(to_near, axis, False), swap(to_far, axis, True)


def call(body, outs, scratch=(), smem=0, extra=1 << 20, cost=None):
    def run(*args):
        held = sum(4 * math.prod(s) for s in outs) + sum(a.size * a.dtype.itemsize for a in args[smem:])
        held += sum(math.prod(s.shape) * 4 for s in scratch)
        grant = held + extra
        specs = [pl.BlockSpec(memory_space=pltpu.SMEM)] * smem
        specs += [pl.BlockSpec(memory_space=pltpu.VMEM)] * (len(args) - smem)
        return pl.pallas_call(
            body,
            out_shape=[jax.ShapeDtypeStruct(s, F32) for s in outs],
            in_specs=specs,
            out_specs=[pl.BlockSpec(memory_space=pltpu.VMEM)] * len(outs),
            scratch_shapes=list(scratch),
            compiler_params=pltpu.CompilerParams(vmem_limit_bytes=grant),
            cost_estimate=cost,
        )(*args)

    return run


class Place:
    def __init__(self, sc, sizes):
        n_row, n_col, rows, cols, rim = sizes
        self.i, self.j = lax.axis_index("row"), lax.axis_index("col")
        self.even_row = self.i % 2 == 0
        self.even_col = self.j % 2 == 0
        self.up = self.i > 0
        self.down = self.i < n_row - 1
        self.has_left = self.j > 0
        self.has_right = self.j < n_col - 1
        self.far_row = jnp.where(self.even_row, self.i, n_row - 1 - self.i) > 0
        self.far_col = jnp.where(self.even_col, self.j, n_col - 1 - self.j) > 0
        if sc is None:
            return
        near = jnp.where(self.even_col, self.j + 1, self.j - 1)
        far = jnp.where(self.even_col, self.j - 1, self.j + 1)
        far = jnp.where(self.far_col, far, self.j)

        spots = sc[...]
        index = lax.broadcasted_iota(jnp.int32, spots.shape, 0) * spots.shape[1]
        index = index + lax.broadcasted_iota(jnp.int32, spots.shape, 1)

        def known(col, part):
            wanted = 2 * (self.i * n_col + col) + part
            return jnp.sum(jnp.where(index == wanted, spots, 0.0)).astype(jnp.int32)

        def row_of(col):
            return pl.multiple_of(known(col, 0) - (self.i * rows - rim), rim // 2)

        self.row = row_of(self.j)
        self.near_row = row_of(near)
        self.far_row_at = row_of(far)
        self.col = known(self.j, 1) - (self.j * cols - rim)


def light_body(sizes, n_dev, sc, pr, pi, out, buf, pw):
    n_row, n_col, rows, cols, rim = sizes
    width = 2 * rim
    half = rim // 2
    power = jnp.sum(pr[...] * pr[...] + pi[...] * pi[...], axis=0)
    lane = lax.broadcasted_iota(jnp.int32, (width, rim), 1)
    a, b = power[:, :rim], power[:, rim:]
    ra, rb = pltpu.roll(a, half, 1), pltpu.roll(b, half, 1)
    zero = jnp.zeros((width, rim), F32)
    pw[0] = jnp.concatenate([a, b, zero], axis=1)
    pw[1] = jnp.concatenate(
        [jnp.where(lane < half, 0.0, ra), jnp.where(lane < half, ra, rb), jnp.where(lane < half, rb, 0.0)],
        axis=1,
    )
    buf[...] = jnp.zeros_like(buf)

    def add(p, carry):
        row = pl.multiple_of(sc[2 * p] + rim, half)
        col = sc[2 * p + 1] + rim
        odd = (col // half) % 2
        at = (pl.ds(row, width), pl.ds(pl.multiple_of(col - odd * half, rim), width + rim))
        buf[at] += pw[odd]
        return carry

    lax.fori_loop(0, n_dev, add, 0)

    def peak_of(k, best):
        at = pl.multiple_of(k * rows + rim, rim)
        return jnp.maximum(best, jnp.max(buf[pl.ds(at, rows), rim : rim + n_col * cols]))

    peak = lax.fori_loop(0, n_row, peak_of, jnp.float32(0.0))
    mine = buf[
        pl.ds(pl.multiple_of(lax.axis_index("row") * rows + rim, rim), rows),
        pl.ds(pl.multiple_of(lax.axis_index("col") * cols + rim, rim), cols),
    ]
    out[...] = mine + light_ratio * peak


def stage_body(*refs):
    count = len(refs) // 2
    ins, outs, sem = refs[:count], refs[count : 2 * count], refs[2 * count]
    copies = [pltpu.make_async_copy(a, b, sem.at[k]) for k, (a, b) in enumerate(zip(ins, outs))]
    for copy in copies:
        copy.start()
    for copy in copies:
        copy.wait()


def stage(*arrays):
    size = sum(a.size * a.dtype.itemsize for a in arrays)
    return pl.pallas_call(
        stage_body,
        out_shape=[jax.ShapeDtypeStruct(a.shape, a.dtype) for a in arrays],
        in_specs=[pl.BlockSpec(memory_space=pltpu.HBM)] * len(arrays),
        out_specs=[pl.BlockSpec(memory_space=pltpu.VMEM)] * len(arrays),
        scratch_shapes=[pltpu.SemaphoreType.DMA((len(arrays),))],
        compiler_params=pltpu.CompilerParams(vmem_limit_bytes=size + (1 << 20)),
        cost_estimate=pl.CostEstimate(flops=0, bytes_accessed=2 * size, transcendentals=0),
    )(*arrays)


def halo_body(sizes, sc, s, near, far, mid, to_near, to_far, ext):
    _, _, rows, _, rim = sizes
    at = Place(sc, sizes)
    width = 2 * rim
    above = jnp.where(at.even_row, far[...], near[...])
    below = jnp.where(at.even_row, near[...], far[...])
    ext[:, :rim] = jnp.where(at.up, above, 0.0)
    ext[:, rim : rim + rows] = s[...]
    ext[:, rim + rows :] = jnp.where(at.down, below, 0.0)
    mid[...] = ext[:, pl.ds(at.row, width)]
    to_near[...] = ext[:, pl.ds(at.near_row, width)]
    to_far[...] = ext[:, pl.ds(at.far_row_at, width)]


def view_body(sizes, last, sc, mid, near, far, pr, pi, view, right_t, left_t, *refs):
    if last:
        gm, to_near, to_far, *parts, spec_scr, win_scr, wave_scr, mix_scr, term_scr = refs
    else:
        gm, to_near, to_far, spec_scr, win_scr, wave_scr, mix_scr = refs
    _, _, _, _, rim = sizes
    at = Place(sc, sizes)
    modes, width = pr.shape[0], pr.shape[1]
    half = rim // 2
    lane = lax.broadcasted_iota(jnp.int32, (width, rim), 1)
    first = at.col == 0
    middle = at.col == half
    for part in range(2):
        a, b = near[part], far[part]
        lft = jnp.where(at.has_left, jnp.where(at.even_col, b, a), 0.0)
        rgt = jnp.where(at.has_right, jnp.where(at.even_col, a, b), 0.0)
        own = mid[part]
        rl, ro, rr = (pltpu.roll(t, half, 1) for t in (lft, own, rgt))
        win_scr[part, :, :rim] = jnp.where(
            first, lft, jnp.where(middle, jnp.where(lane < half, rl, ro), own)
        )
        win_scr[part, :, rim:] = jnp.where(
            first, own, jnp.where(middle, jnp.where(lane < half, ro, rr), rgt)
        )
    for m in range(modes):
        wr, wi = win_scr[0], win_scr[1]
        rows_of = slice(m * width, (m + 1) * width)
        wave_scr[rows_of, :width] = (pr[m] * wr - pi[m] * wi).astype(BF16)
        wave_scr[rows_of, width:] = (pr[m] * wi + pi[m] * wr).astype(BF16)
    mix_scr[...] = jnp.dot(wave_scr[...], right_t[...], preferred_element_type=F32).astype(BF16)
    total = jnp.zeros((width, width), F32)
    for m in range(modes):
        mixed = mix_scr[m * width : (m + 1) * width]
        tall = jnp.concatenate([mixed[:, :width], mixed[:, width:]], axis=0)
        spec = jnp.dot(left_t[...], tall, preferred_element_type=F32)
        spec_scr[m] = spec
        total = total + (spec[:width] * spec[:width] + spec[width:] * spec[width:])
    factor = view[...] / jnp.maximum(jnp.sqrt(total), amp_floor) - 1.0
    for m in range(modes):
        rows_of = slice(m * width, (m + 1) * width)
        wave_scr[rows_of, :width] = (spec_scr[m, :width] * factor).astype(BF16)
        wave_scr[rows_of, width:] = (spec_scr[m, width:] * factor).astype(BF16)
    mix_scr[...] = jnp.dot(wave_scr[...], left_t[...], preferred_element_type=F32).astype(BF16)
    grad = [jnp.zeros((width, width), F32), jnp.zeros((width, width), F32)]
    for m in range(modes):
        mixed = mix_scr[m * width : (m + 1) * width]
        tall = jnp.concatenate([mixed[:, :width], mixed[:, width:]], axis=0)
        back = jnp.dot(right_t[...], tall, preferred_element_type=F32)
        er, ei = back[:width], back[width:]
        grad[0] = grad[0] + (pr[m] * er + pi[m] * ei)
        grad[1] = grad[1] + (pr[m] * ei - pi[m] * er)
        if last:
            wr, wi = win_scr[0], win_scr[1]
            term_scr[m] = wr * er + wi * ei
            term_scr[modes + m] = wr * ei - wi * er
    for part in range(2):
        a, b = grad[part][:, :rim], grad[part][:, rim:]
        ra, rb = pltpu.roll(a, half, 1), pltpu.roll(b, half, 1)
        low = lane < half
        lft = jnp.where(first, a, jnp.where(middle, jnp.where(low, 0.0, ra), 0.0))
        own = jnp.where(first, b, jnp.where(middle, jnp.where(low, ra, rb), a))
        rgt = jnp.where(first, 0.0, jnp.where(middle, jnp.where(low, rb, 0.0), b))
        gm[part] = own
        to_near[part] = jnp.where(at.even_col, rgt, lft)
        to_far[part] = jnp.where(at.even_col, lft, rgt)
    if last:
        wr, wi = win_scr[0], win_scr[1]
        term_scr[2 * modes] = wr * wr + wi * wi
        bit = at.j % 2
        each = parts[0].shape[0]
        for k, part in enumerate(parts):
            at = slice((k // 2) * each, (k // 2 + 1) * each)
            offset = (1 - bit if k % 2 else bit) * rim
            part[...] = term_scr[at, pl.ds(pl.multiple_of(offset, rim), rim)]


def fold_body(sizes, sc, gm, near, far, own, to_near, to_far, buf):
    _, _, rows, _, rim = sizes
    at = Place(sc, sizes)
    width = 2 * rim
    buf[...] = jnp.zeros_like(buf)
    buf[:, pl.ds(at.row, width)] = gm[...]
    buf[:, pl.ds(at.near_row, width)] += near[...]
    buf[:, pl.ds(at.far_row_at, width)] += jnp.where(at.far_col, far[...], 0.0)
    top, bottom = buf[:, :rim], buf[:, rim + rows :]
    own[...] = buf[:, rim : rim + rows]
    to_near[...] = jnp.where(at.even_row, bottom, top)
    to_far[...] = jnp.where(at.even_row, top, bottom)


def step_body(sizes, s, own, near, far, denom, out):
    at = Place(None, sizes)
    grad = own[...] + near[...] + jnp.where(at.far_row, far[...], 0.0)
    out[...] = s[...] + grad / denom[...][None]


def bit_of(axis, level):
    return lax.shift_right_logical(lax.axis_index(("row", "col")[axis]), level) % 2


def halve_body(where, cur, got, keep, send):
    bit = bit_of(*where)
    height = keep.shape[1]
    for out, offset in ((keep, bit * height), (send, (1 - bit) * height)):
        rows = pl.ds(pl.multiple_of(offset, 8), height)
        out[...] = cur[:, rows] + got[:, rows]


def sum_body(cur, got, out):
    out[...] = cur[...] + got[...]


def join_body(where, cur, got, out):
    bit = bit_of(*where)
    height = cur.shape[1]
    for src, offset in ((cur, bit * height), (got, (1 - bit) * height)):
        out[:, pl.ds(pl.multiple_of(offset, 8), height)] = src[...]


def probe_body(rim, *refs):
    colors = (len(refs) - 4) // 2
    mine, got = refs[:colors], refs[colors : 2 * colors]
    pr, pi, new_re, new_im = refs[2 * colors :]
    modes = pr.shape[0]
    each = mine[0].shape[0]
    pixels = 4 * rim * rim
    bit = lax.axis_index("col") % 2

    def term(src, k):
        return src[k // each][k % each]

    mean = (jnp.sum(term(mine, 2 * modes)) + jnp.sum(term(got, 2 * modes))) / pixels
    for src, offset in ((mine, bit * rim), (got, (1 - bit) * rim)):
        rows = pl.ds(pl.multiple_of(offset, rim), rim)
        scale = probe_step / (term(src, 2 * modes) + mass_ratio * mean)
        for m in range(modes):
            new_re[m, rows] = pr[m, rows] + term(src, m) * scale
            new_im[m, rows] = pi[m, rows] + term(src, modes + m) * scale


def swap_bit(array, where):
    axis, level = where
    name = ("row", "col")[axis]
    count = lax.axis_size(name)
    return lax.ppermute(array, name, [(i, i ^ (1 << level)) for i in range(count)])


def sum_terms(keeps, sends, n_row, n_col, beside):
    colors = len(keeps)
    each, height, width = keeps[0].shape
    row_bits = [(0, k) for k in range(n_row.bit_length() - 1)]
    col_bits = [(1, k) for k in range(1, n_col.bit_length() - 1)]
    rest = []
    while row_bits or col_bits:
        if row_bits:
            rest.append(row_bits.pop(0))
        if col_bits:
            rest.append(col_bits.pop(0))
    turn = rest[:colors]
    orders = [turn[c:] + turn[:c] for c in range(colors)]
    tail = rest[colors:]
    curs = list(keeps)
    gots = [swap_bit(a, (1, 0)) for a in sends]
    for r in range(len(turn)):
        height //= 2
        for c in range(colors):
            where = orders[c][r]
            outs = [(each, height, width)] * 2
            keep, send = call(functools.partial(halve_body, where), outs)(curs[c], gots[c])
            curs[c], gots[c] = keep, swap_bit(send, where)
        gots = list(beside(r, gots))
    for k, where in enumerate([None] + tail):
        for c in range(colors):
            (curs[c],) = call(sum_body, [curs[c].shape])(curs[c], gots[c])
            if k < len(tail):
                gots[c] = swap_bit(curs[c], tail[k])
    for r in reversed(range(len(turn))):
        for c in range(colors):
            where = orders[c][r]
            got = swap_bit(curs[c], where)
            outs = [(each, 2 * height, width)]
            (curs[c],) = call(functools.partial(join_body, where), outs)(curs[c], got)
        height *= 2
    return curs, [swap_bit(a, (1, 0)) for a in curs]


def enter_body(n_col, pos, spots):
    at = lax.broadcasted_iota(jnp.int32, spots.shape, 0) * spots.shape[1]
    at = at + lax.broadcasted_iota(jnp.int32, spots.shape, 1)
    me = lax.axis_index("row") * n_col + lax.axis_index("col")
    mine = jnp.where(at == 2 * me, pos[0], jnp.where(at == 2 * me + 1, pos[1], 0))
    spots[...] = mine.astype(F32)


def all_spots(known, n_row, n_col):
    bits = [(1, k) for k in range(n_col.bit_length() - 1)]
    local_bits = len(bits)
    bits += [(0, k) for k in range(n_row.bit_length() - 1)]
    stops = []
    for where in bits:
        known = known + swap_bit(known, where)
        stops.append(known)
    return stops[local_bits - 1], known


def local(obj_re, obj_im, probe_re, probe_im, amps, positions):
    rows, cols = obj_re.shape
    modes, width = probe_re.shape[0], probe_re.shape[1]
    rim = width // 2
    n_row, n_col = lax.axis_size("row"), lax.axis_size("col")
    n_dev = n_row * n_col
    sizes = (n_row, n_col, rows, cols, rim)
    right_np, left_np = tables(width)
    right_t, left_t = jnp.asarray(right_np), jnp.asarray(left_np)
    state = jnp.stack([obj_re, obj_im])
    shape = (-(-2 * n_row * n_col // 128), 128)
    (known,) = call(functools.partial(enter_body, n_col), [shape], smem=1)(positions.reshape(2))
    sc, every = all_spots(known, n_row, n_col)
    view = amps.reshape(width, width)
    staged = stage(probe_re, probe_im, view, right_t, left_t)
    probe_re, probe_im, view, right_t, left_t = staged

    grid = (n_row * rows + 2 * rim, n_col * cols + 3 * rim)
    (denom,) = call(
        functools.partial(light_body, sizes, n_dev),
        [(rows, cols)],
        [pltpu.VMEM(grid, F32), pltpu.VMEM((2, width, width + rim), F32)],
        1,
        extra=4 << 20,
        cost=pl.CostEstimate(flops=8 * n_dev * width * width, bytes_accessed=10**7, transcendentals=0),
    )(every.reshape(-1).astype(jnp.int32), probe_re, probe_im)

    strip = (2, width, cols)
    tile = (2, rows, cols)
    tall = pltpu.VMEM((2, rows + 2 * rim, cols), F32)
    halo = call(functools.partial(halo_body, sizes), [strip] * 3, [tall])
    fold = call(functools.partial(fold_body, sizes), [tile] * 3, [tall])
    step = call(functools.partial(step_body, sizes), [tile])
    scratch = [pltpu.VMEM((modes, 2 * width, width), F32), pltpu.VMEM((2, width, width), F32)]
    scratch += [pltpu.VMEM((modes * width, 2 * width), BF16)] * 2
    terms = ((2 * modes + 1) // COLORS, rim, width)

    for turn in range(ITERS):
        last = turn == ITERS - 1
        near, far = swap_both(state, state, "row")
        mid, to_near, to_far = halo(sc, state, near, far)
        near, far = swap_both(to_near, to_far, "col")
        outs = [strip] * 3 + ([terms] * 2 * COLORS if last else [])
        scr = scratch + ([pltpu.VMEM((2 * modes + 1, width, width), F32)] if last else [])
        res = call(functools.partial(view_body, sizes, last), outs, scr, extra=8 << 20)(
            sc, mid, near, far, probe_re, probe_im, view, right_t, left_t
        )
        gm, to_near, to_far = res[:3]
        near, far = swap_both(to_near, to_far, "col")
        if last:
            break
        own, to_near, to_far = fold(sc, gm, near, far)
        near, far = swap_both(to_near, to_far, "row")
        (state,) = step(state, own, near, far, denom)

    held = {}

    def beside(r, gots):
        if r == 0:
            gots[0], a, b = lax.optimization_barrier((gots[0], near, far))
            held["own"], to_near, to_far = fold(sc, gm, a, b)
            held["both"] = swap_both(to_near, to_far, "row")
        elif r == 1:
            gots[2], a, b = lax.optimization_barrier((gots[2], *held["both"]))
            (held["state"],) = step(state, held["own"], a, b, denom)
        return gots

    mine, other = sum_terms(res[3::2], res[4::2], n_row, n_col, beside)
    shape = (modes, width, width)
    new_re, new_im = call(functools.partial(probe_body, rim), [shape] * 2)(
        *mine, *other, probe_re, probe_im
    )
    return (held["state"][0], held["state"][1], new_re, new_im)


def solution(mesh):
    placed = (
        P("row", "col"),
        P("row", "col"),
        P(),
        P(),
        P("row", "col", None, None, None),
        P("row", "col", None, None),
    )

    return jax.shard_map(
        local,
        mesh=mesh,
        in_specs=placed,
        out_specs=(P("row", "col"), P("row", "col"), P(), P()),
        check_vma=False,
    )
```

```python
import functools
import math

import jax
import jax.numpy as jnp
import numpy as np
from jax import lax
from jax.experimental import pallas as pl
from jax.experimental.pallas import tpu as pltpu
from jax.sharding import PartitionSpec as P


ITERS = 3

amp_floor = 0.25
light_ratio = 0.1
mass_ratio = 0.1
probe_step = 6.0

F32 = jnp.float32
BF16 = jnp.bfloat16
COLORS = 3


def tables(width):
    index = np.arange(width)
    angle = (index[:, None] * index[None, :] % width) * (2.0 * math.pi / width)
    real = (np.cos(angle) / math.sqrt(width)).astype(np.float32)
    imag = (-np.sin(angle) / math.sqrt(width)).astype(np.float32)
    right = np.block([[real, imag], [-imag, real]]).astype(BF16)
    left = np.block([[real, -imag], [imag, real]]).astype(BF16)
    return right, left


def snake(row):
    return row ^ ((row >> 1) & 1)


def work_row():
    row = lax.axis_index("row")
    return snake(row)


def trades():
    return (lax.axis_index("row") >> 1) % 2 == 1


def across(k, far):
    return (k + 1 if k % 2 else k - 1) if far else k ^ 1


def row_pairs(n_row, n_col, far, stored):
    pairs = []
    for row in range(n_row):
        for j in range(n_col):
            other = across(row, far)
            inside = 0 <= other < n_row
            source = other if inside else row
            source = source if stored else snake(source)
            at = j if inside else j ^ 1
            pairs.append((source * n_col + at, snake(row) * n_col + j))
    return sorted(pairs)


def col_pairs(n_row, n_col, far):
    pairs = []
    for i in range(n_row):
        for j in range(n_col):
            other = across(j, far)
            to = (i, other) if 0 <= other < n_col else (i ^ (2 if n_row % 4 == 0 else 1), j)
            pairs.append((i * n_col + j, to[0] * n_col + to[1]))
    return pairs


def trade_pairs(n_row, n_col):
    pairs = []
    for i in range(n_row):
        for j in range(n_col):
            to = (snake(i), j) if snake(i) != i else (i, j ^ 1)
            pairs.append((i * n_col + j, to[0] * n_col + to[1]))
    return pairs


def move(array, pairs):
    return lax.ppermute(array, ("row", "col"), pairs)


def swap(array, axis, far):
    n_row, n_col = lax.axis_size("row"), lax.axis_size("col")
    if axis == "row":
        return move(array, row_pairs(n_row, n_col, far, False))
    return move(array, col_pairs(n_row, n_col, far))


def trade(array):
    return move(array, trade_pairs(lax.axis_size("row"), lax.axis_size("col")))


def swap_both(to_near, to_far, axis):
    return swap(to_near, axis, False), swap(to_far, axis, True)


def call(body, outs, scratch=(), smem=0, extra=1 << 20, cost=None):
    def run(*args):
        held = sum(4 * math.prod(s) for s in outs) + sum(a.size * a.dtype.itemsize for a in args[smem:])
        held += sum(math.prod(s.shape) * 4 for s in scratch)
        grant = held + extra
        specs = [pl.BlockSpec(memory_space=pltpu.SMEM)] * smem
        specs += [pl.BlockSpec(memory_space=pltpu.VMEM)] * (len(args) - smem)
        return pl.pallas_call(
            body,
            out_shape=[jax.ShapeDtypeStruct(s, F32) for s in outs],
            in_specs=specs,
            out_specs=[pl.BlockSpec(memory_space=pltpu.VMEM)] * len(outs),
            scratch_shapes=list(scratch),
            compiler_params=pltpu.CompilerParams(vmem_limit_bytes=grant),
            cost_estimate=cost,
        )(*args)

    return run


class Place:
    def __init__(self, sc, sizes):
        n_row, n_col, rows, cols, rim = sizes
        self.i, self.j = work_row(), lax.axis_index("col")
        self.even_row = self.i % 2 == 0
        self.even_col = self.j % 2 == 0
        self.up = self.i > 0
        self.down = self.i < n_row - 1
        self.has_left = self.j > 0
        self.has_right = self.j < n_col - 1
        self.far_row = jnp.where(self.even_row, self.i, n_row - 1 - self.i) > 0
        self.far_col = jnp.where(self.even_col, self.j, n_col - 1 - self.j) > 0
        if sc is None:
            return
        near = jnp.where(self.even_col, self.j + 1, self.j - 1)
        far = jnp.where(self.even_col, self.j - 1, self.j + 1)
        far = jnp.where(self.far_col, far, self.j)

        spots = sc[...]
        index = lax.broadcasted_iota(jnp.int32, spots.shape, 0) * spots.shape[1]
        index = index + lax.broadcasted_iota(jnp.int32, spots.shape, 1)

        def known(col, part):
            wanted = 2 * (self.i * n_col + col) + part
            return jnp.sum(jnp.where(index == wanted, spots, 0.0)).astype(jnp.int32)

        def row_of(col):
            return pl.multiple_of(known(col, 0) - (self.i * rows - rim), rim // 2)

        self.row = row_of(self.j)
        self.near_row = row_of(near)
        self.far_row_at = row_of(far)
        self.col = known(self.j, 1) - (self.j * cols - rim)


def light_body(sizes, n_dev, sc, pr, pi, out, buf, pw):
    n_row, n_col, rows, cols, rim = sizes
    width = 2 * rim
    half = rim // 2
    power = jnp.sum(pr[...] * pr[...] + pi[...] * pi[...], axis=0)
    lane = lax.broadcasted_iota(jnp.int32, (width, rim), 1)
    a, b = power[:, :rim], power[:, rim:]
    ra, rb = pltpu.roll(a, half, 1), pltpu.roll(b, half, 1)
    zero = jnp.zeros((width, rim), F32)
    pw[0] = jnp.concatenate([a, b, zero], axis=1)
    pw[1] = jnp.concatenate(
        [jnp.where(lane < half, 0.0, ra), jnp.where(lane < half, ra, rb), jnp.where(lane < half, rb, 0.0)],
        axis=1,
    )
    buf[...] = jnp.zeros_like(buf)

    def add(p, carry):
        row = pl.multiple_of(sc[2 * p] + rim, half)
        col = sc[2 * p + 1] + rim
        odd = (col // half) % 2
        at = (pl.ds(row, width), pl.ds(pl.multiple_of(col - odd * half, rim), width + rim))
        buf[at] += pw[odd]
        return carry

    lax.fori_loop(0, n_dev, add, 0)

    def peak_of(k, best):
        at = pl.multiple_of(k * rows + rim, rim)
        return jnp.maximum(best, jnp.max(buf[pl.ds(at, rows), rim : rim + n_col * cols]))

    peak = lax.fori_loop(0, n_row, peak_of, jnp.float32(0.0))
    mine = buf[
        pl.ds(pl.multiple_of(work_row() * rows + rim, rim), rows),
        pl.ds(pl.multiple_of(lax.axis_index("col") * cols + rim, rim), cols),
    ]
    out[...] = mine + light_ratio * peak


def stage_body(*refs):
    count = len(refs) // 2
    ins, outs, sem = refs[:count], refs[count : 2 * count], refs[2 * count]
    copies = [pltpu.make_async_copy(a, b, sem.at[k]) for k, (a, b) in enumerate(zip(ins, outs))]
    for copy in copies:
        copy.start()
    for copy in copies:
        copy.wait()


def stage(*arrays):
    arrays = [pltpu.with_memory_space_constraint(a, pltpu.HBM) for a in arrays]
    size = sum(a.size * a.dtype.itemsize for a in arrays)
    return pl.pallas_call(
        stage_body,
        out_shape=[jax.ShapeDtypeStruct(a.shape, a.dtype) for a in arrays],
        in_specs=[pl.BlockSpec(memory_space=pltpu.HBM)] * len(arrays),
        out_specs=[pl.BlockSpec(memory_space=pltpu.VMEM)] * len(arrays),
        scratch_shapes=[pltpu.SemaphoreType.DMA((len(arrays),))],
        compiler_params=pltpu.CompilerParams(vmem_limit_bytes=size + (1 << 20)),
        cost_estimate=pl.CostEstimate(flops=0, bytes_accessed=2 * size, transcendentals=0),
    )(*arrays)


def first_halo_body(sizes, s, near, far, out, own):
    _, _, rows, _, rim = sizes
    at = Place(None, sizes)
    here = jnp.where(trades(), near[...], s[...])
    beside = jnp.where(trades(), s[...], near[...])
    above = jnp.where(at.even_row, far[...], beside)
    below = jnp.where(at.even_row, beside, far[...])
    own[...] = here
    out[:, :rim] = jnp.where(at.up, above, 0.0)
    out[:, rim : rim + rows] = here
    out[:, rim + rows :] = jnp.where(at.down, below, 0.0)


def halo_body(sizes, sc, s, near, far, mid, to_near, to_far, ext):
    _, _, rows, _, rim = sizes
    at = Place(sc, sizes)
    width = 2 * rim
    above = jnp.where(at.even_row, far[...], near[...])
    below = jnp.where(at.even_row, near[...], far[...])
    ext[:, :rim] = jnp.where(at.up, above, 0.0)
    ext[:, rim : rim + rows] = s[...]
    ext[:, rim + rows :] = jnp.where(at.down, below, 0.0)
    mid[...] = ext[:, pl.ds(at.row, width)]
    to_near[...] = ext[:, pl.ds(at.near_row, width)]
    to_far[...] = ext[:, pl.ds(at.far_row_at, width)]


def view_body(sizes, last, sc, mid, near, far, pr, pi, view, traded, right_t, left_t, *refs):
    if last:
        gm, to_near, to_far, *parts, spec_scr, win_scr, wave_scr, mix_scr, term_scr = refs
    else:
        gm, to_near, to_far, spec_scr, win_scr, wave_scr, mix_scr = refs
    _, _, _, _, rim = sizes
    at = Place(sc, sizes)
    modes, width = pr.shape[0], pr.shape[1]
    half = rim // 2
    lane = lax.broadcasted_iota(jnp.int32, (width, rim), 1)
    first = at.col == 0
    middle = at.col == half
    for part in range(2):
        rows_of = pl.ds(at.row, width) if mid.shape[1] > width else slice(None)
        a, b = near[part, rows_of], far[part, rows_of]
        lft = jnp.where(at.has_left, jnp.where(at.even_col, b, a), 0.0)
        rgt = jnp.where(at.has_right, jnp.where(at.even_col, a, b), 0.0)
        own = mid[part, rows_of]
        rl, ro, rr = (pltpu.roll(t, half, 1) for t in (lft, own, rgt))
        win_scr[part, :, :rim] = jnp.where(
            first, lft, jnp.where(middle, jnp.where(lane < half, rl, ro), own)
        )
        win_scr[part, :, rim:] = jnp.where(
            first, own, jnp.where(middle, jnp.where(lane < half, ro, rr), rgt)
        )
    for m in range(modes):
        wr, wi = win_scr[0], win_scr[1]
        rows_of = slice(m * width, (m + 1) * width)
        wave_scr[rows_of, :width] = (pr[m] * wr - pi[m] * wi).astype(BF16)
        wave_scr[rows_of, width:] = (pr[m] * wi + pi[m] * wr).astype(BF16)
    mix_scr[...] = jnp.dot(wave_scr[...], right_t[...], preferred_element_type=F32).astype(BF16)
    total = jnp.zeros((width, width), F32)
    for m in range(modes):
        mixed = mix_scr[m * width : (m + 1) * width]
        tall = jnp.concatenate([mixed[:, :width], mixed[:, width:]], axis=0)
        spec = jnp.dot(left_t[...], tall, preferred_element_type=F32)
        spec_scr[m] = spec
        total = total + (spec[:width] * spec[:width] + spec[width:] * spec[width:])
    amps = jnp.where(trades(), traded[...], view[...])
    factor = amps / jnp.maximum(jnp.sqrt(total), amp_floor) - 1.0
    for m in range(modes):
        rows_of = slice(m * width, (m + 1) * width)
        wave_scr[rows_of, :width] = (spec_scr[m, :width] * factor).astype(BF16)
        wave_scr[rows_of, width:] = (spec_scr[m, width:] * factor).astype(BF16)
    mix_scr[...] = jnp.dot(wave_scr[...], left_t[...], preferred_element_type=F32).astype(BF16)
    grad = [jnp.zeros((width, width), F32), jnp.zeros((width, width), F32)]
    for m in range(modes):
        mixed = mix_scr[m * width : (m + 1) * width]
        tall = jnp.concatenate([mixed[:, :width], mixed[:, width:]], axis=0)
        back = jnp.dot(right_t[...], tall, preferred_element_type=F32)
        er, ei = back[:width], back[width:]
        grad[0] = grad[0] + (pr[m] * er + pi[m] * ei)
        grad[1] = grad[1] + (pr[m] * ei - pi[m] * er)
        if last:
            wr, wi = win_scr[0], win_scr[1]
            term_scr[m] = wr * er + wi * ei
            term_scr[modes + m] = wr * ei - wi * er
    for part in range(2):
        a, b = grad[part][:, :rim], grad[part][:, rim:]
        ra, rb = pltpu.roll(a, half, 1), pltpu.roll(b, half, 1)
        low = lane < half
        lft = jnp.where(first, a, jnp.where(middle, jnp.where(low, 0.0, ra), 0.0))
        own = jnp.where(first, b, jnp.where(middle, jnp.where(low, ra, rb), a))
        rgt = jnp.where(first, 0.0, jnp.where(middle, jnp.where(low, rb, 0.0), b))
        gm[part] = own
        to_near[part] = jnp.where(at.even_col, rgt, lft)
        to_far[part] = jnp.where(at.even_col, lft, rgt)
    if last:
        wr, wi = win_scr[0], win_scr[1]
        term_scr[2 * modes] = wr * wr + wi * wi
        bit = at.j % 2
        each = parts[0].shape[0]
        for k, part in enumerate(parts):
            at = slice((k // 2) * each, (k // 2 + 1) * each)
            offset = (1 - bit if k % 2 else bit) * rim
            part[...] = term_scr[at, pl.ds(pl.multiple_of(offset, rim), rim)]


def fold_body(sizes, sc, gm, near, far, own, to_near, to_far, buf):
    _, _, rows, _, rim = sizes
    at = Place(sc, sizes)
    width = 2 * rim
    buf[...] = jnp.zeros_like(buf)
    buf[:, pl.ds(at.row, width)] = gm[...]
    buf[:, pl.ds(at.near_row, width)] += near[...]
    buf[:, pl.ds(at.far_row_at, width)] += jnp.where(at.far_col, far[...], 0.0)
    top, bottom = buf[:, :rim], buf[:, rim + rows :]
    own[...] = buf[:, rim : rim + rows]
    to_near[...] = jnp.where(at.even_row, bottom, top)
    to_far[...] = jnp.where(at.even_row, top, bottom)


def step_body(sizes, s, own, near, far, denom, out):
    at = Place(None, sizes)
    grad = own[...] + near[...] + jnp.where(at.far_row, far[...], 0.0)
    out[...] = s[...] + grad / denom[...][None]


def leave_body(state, traded, out_re, out_im):
    for k, out in enumerate((out_re, out_im)):
        out[...] = jnp.where(trades(), traded[k], state[k])


def bit_of(axis, level):
    return lax.shift_right_logical(lax.axis_index(("row", "col")[axis]), level) % 2


def halve_body(where, cur, got, keep, send):
    bit = bit_of(*where)
    height = keep.shape[1]
    for out, offset in ((keep, bit * height), (send, (1 - bit) * height)):
        rows = pl.ds(pl.multiple_of(offset, 8), height)
        out[...] = cur[:, rows] + got[:, rows]


def sum_body(cur, got, out):
    out[...] = cur[...] + got[...]


def join_body(where, cur, got, out):
    bit = bit_of(*where)
    height = cur.shape[1]
    for src, offset in ((cur, bit * height), (got, (1 - bit) * height)):
        out[:, pl.ds(pl.multiple_of(offset, 8), height)] = src[...]


def probe_body(rim, *refs):
    colors = (len(refs) - 4) // 2
    mine, got = refs[:colors], refs[colors : 2 * colors]
    pr, pi, new_re, new_im = refs[2 * colors :]
    modes = pr.shape[0]
    each = mine[0].shape[0]
    pixels = 4 * rim * rim
    bit = lax.axis_index("col") % 2

    def term(src, k):
        return src[k // each][k % each]

    mean = (jnp.sum(term(mine, 2 * modes)) + jnp.sum(term(got, 2 * modes))) / pixels
    for src, offset in ((mine, bit * rim), (got, (1 - bit) * rim)):
        rows = pl.ds(pl.multiple_of(offset, rim), rim)
        scale = probe_step / (term(src, 2 * modes) + mass_ratio * mean)
        for m in range(modes):
            new_re[m, rows] = pr[m, rows] + term(src, m) * scale
            new_im[m, rows] = pi[m, rows] + term(src, modes + m) * scale


def swap_bit(array, where):
    axis, level = where
    name = ("row", "col")[axis]
    count = lax.axis_size(name)
    return lax.ppermute(array, name, [(i, i ^ (1 << level)) for i in range(count)])


def sum_terms(keeps, sends, n_row, n_col, beside, late):
    colors = len(keeps)
    each, height, width = keeps[0].shape
    row_bits = [(0, k) for k in range(n_row.bit_length() - 1)]
    col_bits = [(1, k) for k in range(1, n_col.bit_length() - 1)]
    rest = []
    while row_bits or col_bits:
        if row_bits:
            rest.append(row_bits.pop(0))
        if col_bits:
            rest.append(col_bits.pop(0))
    turn = rest[:colors]
    orders = [turn[c:] + turn[:c] for c in range(colors)]
    tail = rest[colors:]
    curs = list(keeps)
    gots = [swap_bit(a, (1, 0)) for a in sends]
    for r in range(len(turn)):
        height //= 2
        for c in range(colors):
            where = orders[c][r]
            outs = [(each, height, width)] * 2
            keep, send = call(functools.partial(halve_body, where), outs)(curs[c], gots[c])
            curs[c], gots[c] = keep, swap_bit(send, where)
        gots = list(beside(r, gots))
    for k, where in enumerate([None] + tail):
        for c in range(colors):
            (curs[c],) = call(sum_body, [curs[c].shape])(curs[c], gots[c])
            if k < len(tail):
                gots[c] = swap_bit(curs[c], tail[k])
    for r in reversed(range(len(turn))):
        for c in range(colors):
            where = orders[c][r]
            got = swap_bit(curs[c], where)
            if c == 0 and r == len(turn) - 2:
                got = late(got)
            outs = [(each, 2 * height, width)]
            (curs[c],) = call(functools.partial(join_body, where), outs)(curs[c], got)
        height *= 2
    return curs, [swap_bit(a, (1, 0)) for a in curs]


def enter_body(n_col, pos, spots):
    at = lax.broadcasted_iota(jnp.int32, spots.shape, 0) * spots.shape[1]
    at = at + lax.broadcasted_iota(jnp.int32, spots.shape, 1)
    me = lax.axis_index("row") * n_col + lax.axis_index("col")
    mine = jnp.where(at == 2 * me, pos[0], jnp.where(at == 2 * me + 1, pos[1], 0))
    spots[...] = mine.astype(F32)


def spot_bits(n_row, n_col):
    bits = [(0, 0)] + [(1, k) for k in range(n_col.bit_length() - 1)]
    return bits + [(0, k) for k in range(1, n_row.bit_length() - 1)]


def gather_spots(known, bits):
    stops = []
    for where in bits:
        known = known + swap_bit(known, where)
        stops.append(known)
    return stops


def local(obj_re, obj_im, probe_re, probe_im, amps, positions):
    rows, cols = obj_re.shape
    modes, width = probe_re.shape[0], probe_re.shape[1]
    rim = width // 2
    n_row, n_col = lax.axis_size("row"), lax.axis_size("col")
    n_dev = n_row * n_col
    sizes = (n_row, n_col, rows, cols, rim)
    right_np, left_np = tables(width)
    right_t, left_t = jnp.asarray(right_np), jnp.asarray(left_np)
    state = jnp.stack([obj_re, obj_im])
    shape = (-(-2 * n_row * n_col // 128), 128)
    (known,) = call(functools.partial(enter_body, n_col), [shape], smem=1)(positions.reshape(2))
    bits = spot_bits(n_row, n_col)
    local_bits = n_col.bit_length()
    stops = gather_spots(known, bits[:local_bits])
    view = amps.reshape(width, width)
    traded = trade(view)
    staged = stage(probe_re, probe_im, view, right_t, left_t)
    probe_re, probe_im, view, right_t, left_t = staged

    grid = (n_row * rows + 2 * rim, n_col * cols + 3 * rim)
    light = call(
        functools.partial(light_body, sizes, n_dev),
        [(rows, cols)],
        [pltpu.VMEM(grid, F32), pltpu.VMEM((2, width, width + rim), F32)],
        1,
        extra=4 << 20,
        cost=pl.CostEstimate(flops=8 * n_dev * width * width, bytes_accessed=10**7, transcendentals=0),
    )

    strip = (2, width, cols)
    tile = (2, rows, cols)
    tall = pltpu.VMEM((2, rows + 2 * rim, cols), F32)
    first_halo = call(functools.partial(first_halo_body, sizes), [(2, rows + 2 * rim, cols), tile])
    halo = call(functools.partial(halo_body, sizes), [strip] * 3, [tall])
    fold = call(functools.partial(fold_body, sizes), [tile] * 3, [tall])
    step = call(functools.partial(step_body, sizes), [tile])
    scratch = [pltpu.VMEM((modes, 2 * width, width), F32), pltpu.VMEM((2, width, width), F32)]
    scratch += [pltpu.VMEM((modes * width, 2 * width), BF16)] * 2
    terms = ((2 * modes + 1) // COLORS, rim, width)

    for turn in range(ITERS):
        last = turn == ITERS - 1
        if turn == 0:
            near = swap(state, "row", False)
            far = move(state, row_pairs(n_row, n_col, True, True))
            near, far, sc = lax.optimization_barrier((near, far, stops[-1]))
            most = gather_spots(sc, bits[local_bits:-1])[-1]
            mid, state = first_halo(state, near, far)
            to_near = to_far = mid
        else:
            near, far = swap_both(state, state, "row")
            mid, to_near, to_far = halo(sc, state, near, far)
        near, far = swap_both(to_near, to_far, "col")
        if turn == 0:
            near, far, most = lax.optimization_barrier((near, far, most))
            every = gather_spots(most, bits[-1:])[-1]
            (denom,) = light(every.reshape(-1).astype(jnp.int32), probe_re, probe_im)
        outs = [strip] * 3 + ([terms] * 2 * COLORS if last else [])
        scr = scratch + ([pltpu.VMEM((2 * modes + 1, width, width), F32)] if last else [])
        res = call(functools.partial(view_body, sizes, last), outs, scr, extra=8 << 20)(
            sc, mid, near, far, probe_re, probe_im, view, traded, right_t, left_t
        )
        gm, to_near, to_far = res[:3]
        near, far = swap_both(to_near, to_far, "col")
        if last:
            break
        own, to_near, to_far = fold(sc, gm, near, far)
        near, far = swap_both(to_near, to_far, "row")
        (state,) = step(state, own, near, far, denom)

    held = {}

    def beside(r, gots):
        if r == 0:
            gots[0], a, b = lax.optimization_barrier((gots[0], near, far))
            held["own"], to_near, to_far = fold(sc, gm, a, b)
            held["both"] = swap_both(to_near, to_far, "row")
        elif r == 1:
            gots[2], a, b = lax.optimization_barrier((gots[2], *held["both"]))
            (held["state"],) = step(state, held["own"], a, b, denom)
            held["traded"] = trade(held["state"])
        return gots

    def late(got):
        got, held["traded"], held["state"] = lax.optimization_barrier(
            (got, held["traded"], held["state"])
        )
        return got

    mine, other = sum_terms(res[3::2], res[4::2], n_row, n_col, beside, late)
    shape = (modes, width, width)
    new_re, new_im = call(functools.partial(probe_body, rim), [shape] * 2)(
        *mine, *other, probe_re, probe_im
    )
    done_re, done_im = call(leave_body, [(rows, cols)] * 2)(held["state"], held["traded"])
    return (done_re, done_im, new_re, new_im)


def solution(mesh):
    placed = (
        P("row", "col"),
        P("row", "col"),
        P(),
        P(),
        P("row", "col", None, None, None),
        P("row", "col", None, None),
    )

    return jax.shard_map(
        local,
        mesh=mesh,
        in_specs=placed,
        out_specs=(P("row", "col"), P("row", "col"), P(), P()),
        check_vma=False,
    )
```

```python
import functools
import math

import jax
import jax.numpy as jnp
import numpy as np
from jax import lax
from jax.experimental import pallas as pl
from jax.experimental.pallas import tpu as pltpu
from jax.sharding import PartitionSpec as P


ITERS = 3

amp_floor = 0.25
light_ratio = 0.1
mass_ratio = 0.1
probe_step = 6.0

F32 = jnp.float32
BF16 = jnp.bfloat16
COLORS = 3


def tables(width):
    half = width // 2
    angle = (np.arange(half)[:, None] * np.arange(width)[None, :] % width) * (2.0 * math.pi / width)
    real = np.cos(angle) / math.sqrt(width)
    imag = -np.sin(angle) / math.sqrt(width)
    pairs = []
    for k in range(2):
        re, im = real[:, k::2], imag[:, k::2]
        pairs.append(np.block([[re, im], [-im, re]]))
    return np.stack(pairs + [p.T for p in pairs]).astype(np.float32).astype(BF16)


def sort_body(view, out):
    width = view.shape[0]
    half = width // 2
    row = lax.broadcasted_iota(jnp.int32, (width, width), 0)
    col = lax.broadcasted_iota(jnp.int32, (width, width), 1)

    def source(k):
        return jnp.where(k < half, 2 * k, 2 * (k - half) + 1)

    def picked(left, rows):
        pick = jnp.where(col == source(row) if rows else row == source(col), 1.0, 0.0).astype(BF16)
        total = jnp.zeros((width, width), F32)
        for _ in range(3):
            part = left.astype(BF16)
            left = left - part.astype(F32)
            pair = (pick, part) if rows else (part, pick)
            total = total + jnp.dot(*pair, preferred_element_type=F32)
        return total

    out[...] = picked(picked(view[...], True), False)


def snake(row):
    return row ^ ((row >> 1) & 1)


def work_row():
    row = lax.axis_index("row")
    return snake(row)


def trades():
    return (lax.axis_index("row") >> 1) % 2 == 1


def across(k, far):
    return (k + 1 if k % 2 else k - 1) if far else k ^ 1


def row_pairs(n_row, n_col, far, stored):
    pairs = []
    for row in range(n_row):
        for j in range(n_col):
            other = across(row, far)
            inside = 0 <= other < n_row
            source = other if inside else row
            source = source if stored else snake(source)
            at = j if inside else j ^ 1
            pairs.append((source * n_col + at, snake(row) * n_col + j))
    return sorted(pairs)


def col_pairs(n_row, n_col, far):
    pairs = []
    for i in range(n_row):
        for j in range(n_col):
            other = across(j, far)
            to = (i, other) if 0 <= other < n_col else (i ^ (2 if n_row % 4 == 0 else 1), j)
            pairs.append((i * n_col + j, to[0] * n_col + to[1]))
    return pairs


def trade_pairs(n_row, n_col):
    pairs = []
    for i in range(n_row):
        for j in range(n_col):
            to = (snake(i), j) if snake(i) != i else (i, j ^ 1)
            pairs.append((i * n_col + j, to[0] * n_col + to[1]))
    return pairs


def move(array, pairs):
    return lax.ppermute(array, ("row", "col"), pairs)


def swap(array, axis, far):
    n_row, n_col = lax.axis_size("row"), lax.axis_size("col")
    if axis == "row":
        return move(array, row_pairs(n_row, n_col, far, False))
    return move(array, col_pairs(n_row, n_col, far))


def trade(array):
    return move(array, trade_pairs(lax.axis_size("row"), lax.axis_size("col")))


def swap_both(to_near, to_far, axis):
    return swap(to_near, axis, False), swap(to_far, axis, True)


def call(body, outs, scratch=(), smem=0, extra=1 << 20, cost=None):
    def run(*args):
        held = sum(4 * math.prod(s) for s in outs) + sum(a.size * a.dtype.itemsize for a in args[smem:])
        held += sum(math.prod(s.shape) * 4 for s in scratch)
        grant = held + extra
        specs = [pl.BlockSpec(memory_space=pltpu.SMEM)] * smem
        specs += [pl.BlockSpec(memory_space=pltpu.VMEM)] * (len(args) - smem)
        return pl.pallas_call(
            body,
            out_shape=[jax.ShapeDtypeStruct(s, F32) for s in outs],
            in_specs=specs,
            out_specs=[pl.BlockSpec(memory_space=pltpu.VMEM)] * len(outs),
            scratch_shapes=list(scratch),
            compiler_params=pltpu.CompilerParams(vmem_limit_bytes=grant),
            cost_estimate=cost,
        )(*args)

    return run


class Place:
    def __init__(self, sc, sizes):
        n_row, n_col, rows, cols, rim = sizes
        self.i, self.j = work_row(), lax.axis_index("col")
        self.even_row = self.i % 2 == 0
        self.even_col = self.j % 2 == 0
        self.up = self.i > 0
        self.down = self.i < n_row - 1
        self.has_left = self.j > 0
        self.has_right = self.j < n_col - 1
        self.far_row = jnp.where(self.even_row, self.i, n_row - 1 - self.i) > 0
        self.far_col = jnp.where(self.even_col, self.j, n_col - 1 - self.j) > 0
        if sc is None:
            return
        near = jnp.where(self.even_col, self.j + 1, self.j - 1)
        far = jnp.where(self.even_col, self.j - 1, self.j + 1)
        far = jnp.where(self.far_col, far, self.j)

        spots = sc[...]
        index = lax.broadcasted_iota(jnp.int32, spots.shape, 0) * spots.shape[1]
        index = index + lax.broadcasted_iota(jnp.int32, spots.shape, 1)

        def known(col, part):
            wanted = 2 * (self.i * n_col + col) + part
            return jnp.sum(jnp.where(index == wanted, spots, 0.0)).astype(jnp.int32)

        def row_of(col):
            return pl.multiple_of(known(col, 0) - (self.i * rows - rim), rim // 2)

        self.row = row_of(self.j)
        self.near_row = row_of(near)
        self.far_row_at = row_of(far)
        self.col = known(self.j, 1) - (self.j * cols - rim)


def light_body(sizes, n_dev, sc, pr, pi, out, buf, pw):
    n_row, n_col, rows, cols, rim = sizes
    width = 2 * rim
    half = rim // 2
    power = jnp.sum(pr[...] * pr[...] + pi[...] * pi[...], axis=0)
    lane = lax.broadcasted_iota(jnp.int32, (width, rim), 1)
    a, b = power[:, :rim], power[:, rim:]
    ra, rb = pltpu.roll(a, half, 1), pltpu.roll(b, half, 1)
    zero = jnp.zeros((width, rim), F32)
    pw[0] = jnp.concatenate([a, b, zero], axis=1)
    pw[1] = jnp.concatenate(
        [jnp.where(lane < half, 0.0, ra), jnp.where(lane < half, ra, rb), jnp.where(lane < half, rb, 0.0)],
        axis=1,
    )
    buf[...] = jnp.zeros_like(buf)

    def add(p, carry):
        row = pl.multiple_of(sc[2 * p] + rim, half)
        col = sc[2 * p + 1] + rim
        odd = (col // half) % 2
        at = (pl.ds(row, width), pl.ds(pl.multiple_of(col - odd * half, rim), width + rim))
        buf[at] += pw[odd]
        return carry

    lax.fori_loop(0, n_dev, add, 0)

    def peak_of(k, best):
        at = pl.multiple_of(k * rows + rim, rim)
        return jnp.maximum(best, jnp.max(buf[pl.ds(at, rows), rim : rim + n_col * cols]))

    peak = lax.fori_loop(0, n_row, peak_of, jnp.float32(0.0))
    mine = buf[
        pl.ds(pl.multiple_of(work_row() * rows + rim, rim), rows),
        pl.ds(pl.multiple_of(lax.axis_index("col") * cols + rim, rim), cols),
    ]
    out[...] = mine + light_ratio * peak


def stage_body(*refs):
    count = len(refs) // 2
    ins, outs, sem = refs[:count], refs[count : 2 * count], refs[2 * count]
    copies = [pltpu.make_async_copy(a, b, sem.at[k]) for k, (a, b) in enumerate(zip(ins, outs))]
    for copy in copies:
        copy.start()
    for copy in copies:
        copy.wait()


def stage(*arrays):
    arrays = [pltpu.with_memory_space_constraint(a, pltpu.HBM) for a in arrays]
    size = sum(a.size * a.dtype.itemsize for a in arrays)
    return pl.pallas_call(
        stage_body,
        out_shape=[jax.ShapeDtypeStruct(a.shape, a.dtype) for a in arrays],
        in_specs=[pl.BlockSpec(memory_space=pltpu.HBM)] * len(arrays),
        out_specs=[pl.BlockSpec(memory_space=pltpu.VMEM)] * len(arrays),
        scratch_shapes=[pltpu.SemaphoreType.DMA((len(arrays),))],
        compiler_params=pltpu.CompilerParams(vmem_limit_bytes=size + (1 << 20)),
        cost_estimate=pl.CostEstimate(flops=0, bytes_accessed=2 * size, transcendentals=0),
    )(*arrays)


def first_halo_body(sizes, s, near, far, out, own):
    _, _, rows, _, rim = sizes
    at = Place(None, sizes)
    here = jnp.where(trades(), near[...], s[...])
    beside = jnp.where(trades(), s[...], near[...])
    above = jnp.where(at.even_row, far[...], beside)
    below = jnp.where(at.even_row, beside, far[...])
    own[...] = here
    out[:, :rim] = jnp.where(at.up, above, 0.0)
    out[:, rim : rim + rows] = here
    out[:, rim + rows :] = jnp.where(at.down, below, 0.0)


def halo_body(sizes, sc, s, near, far, mid, to_near, to_far, ext):
    _, _, rows, _, rim = sizes
    at = Place(sc, sizes)
    width = 2 * rim
    above = jnp.where(at.even_row, far[...], near[...])
    below = jnp.where(at.even_row, near[...], far[...])
    ext[:, :rim] = jnp.where(at.up, above, 0.0)
    ext[:, rim : rim + rows] = s[...]
    ext[:, rim + rows :] = jnp.where(at.down, below, 0.0)
    mid[...] = ext[:, pl.ds(at.row, width)]
    to_near[...] = ext[:, pl.ds(at.near_row, width)]
    to_far[...] = ext[:, pl.ds(at.far_row_at, width)]


def view_body(sizes, last, sc, mid, near, far, pr, pi, view, traded, tabs, *refs):
    if last:
        gm, to_near, to_far, *parts, spec_scr, win_scr, wave_e, wave_o, mix_e, mix_o, term_scr = refs
    else:
        gm, to_near, to_far, spec_scr, win_scr, wave_e, wave_o, mix_e, mix_o = refs
    _, _, _, _, rim = sizes
    at = Place(sc, sizes)
    modes, width = pr.shape[0], pr.shape[1]
    half = rim // 2
    lane = lax.broadcasted_iota(jnp.int32, (width, rim), 1)
    first = at.col == 0
    middle = at.col == half
    for part in range(2):
        rows_of = pl.ds(at.row, width) if mid.shape[1] > width else slice(None)
        a, b = near[part, rows_of], far[part, rows_of]
        lft = jnp.where(at.has_left, jnp.where(at.even_col, b, a), 0.0)
        rgt = jnp.where(at.has_right, jnp.where(at.even_col, a, b), 0.0)
        own = mid[part, rows_of]
        rl, ro, rr = (pltpu.roll(t, half, 1) for t in (lft, own, rgt))
        win_scr[part, :, :rim] = jnp.where(
            first, lft, jnp.where(middle, jnp.where(lane < half, rl, ro), own)
        )
        win_scr[part, :, rim:] = jnp.where(
            first, own, jnp.where(middle, jnp.where(lane < half, ro, rr), rgt)
        )
    even, odd, even_t, odd_t = range(4)
    for m in range(modes):
        wr, wi = win_scr[0], win_scr[1]
        here = slice(m * width, (m + 1) * width)
        for k, psi in enumerate((pr[m] * wr - pi[m] * wi, pr[m] * wi + pi[m] * wr)):
            lanes = slice(k * rim, (k + 1) * rim)
            wave_e[here, lanes] = (psi[:, :rim] + psi[:, rim:]).astype(BF16)
            wave_o[here, lanes] = (psi[:, :rim] - psi[:, rim:]).astype(BF16)
    mix_e[...] = jnp.dot(wave_e[...], tabs[even], preferred_element_type=F32)
    mix_o[...] = jnp.dot(wave_o[...], tabs[odd], preferred_element_type=F32)
    total = [jnp.zeros((rim, width), F32), jnp.zeros((rim, width), F32)]
    for m in range(modes):
        top, low = slice(m * width, m * width + rim), slice(m * width + rim, (m + 1) * width)
        for k, sign in ((0, 1.0), (1, -1.0)):
            e = mix_e[top] + sign * mix_e[low]
            o = mix_o[top] + sign * mix_o[low]
            tall = jnp.concatenate(
                [
                    jnp.concatenate([e[:, :rim], o[:, :rim]], axis=1),
                    jnp.concatenate([e[:, rim:], o[:, rim:]], axis=1),
                ],
                axis=0,
            ).astype(BF16)
            spec = jnp.dot(tabs[even_t + k], tall, preferred_element_type=F32)
            spec_scr[m, k] = spec
            total[k] = total[k] + (spec[:rim] * spec[:rim] + spec[rim:] * spec[rim:])
    for k in range(2):
        band = slice(k * rim, (k + 1) * rim)
        amps = jnp.where(trades(), traded[band], view[band])
        factor = amps / jnp.maximum(jnp.sqrt(total[k]), amp_floor) - 1.0
        for m in range(modes):
            here = slice((2 * m + k) * rim, (2 * m + k + 1) * rim)
            for part in range(2):
                lanes = slice(part * rim, (part + 1) * rim)
                change = spec_scr[m, k, lanes] * factor
                wave_e[here, lanes] = change[:, :rim].astype(BF16)
                wave_o[here, lanes] = change[:, rim:].astype(BF16)
    mix_e[...] = jnp.dot(wave_e[...], tabs[even_t], preferred_element_type=F32)
    mix_o[...] = jnp.dot(wave_o[...], tabs[odd_t], preferred_element_type=F32)
    grad = [jnp.zeros((width, width), F32), jnp.zeros((width, width), F32)]
    for m in range(modes):
        ends = []
        for k in range(2):
            here = slice((2 * m + k) * rim, (2 * m + k + 1) * rim)
            plus, minus = mix_e[here] + mix_o[here], mix_e[here] - mix_o[here]
            tall = jnp.concatenate(
                [
                    jnp.concatenate([plus[:, :rim], minus[:, :rim]], axis=1),
                    jnp.concatenate([plus[:, rim:], minus[:, rim:]], axis=1),
                ],
                axis=0,
            ).astype(BF16)
            ends.append(jnp.dot(tabs[even + k], tall, preferred_element_type=F32))
        plus, minus = ends[0] + ends[1], ends[0] - ends[1]
        er = jnp.concatenate([plus[:rim], minus[:rim]], axis=0)
        ei = jnp.concatenate([plus[rim:], minus[rim:]], axis=0)
        grad[0] = grad[0] + (pr[m] * er + pi[m] * ei)
        grad[1] = grad[1] + (pr[m] * ei - pi[m] * er)
        if last:
            wr, wi = win_scr[0], win_scr[1]
            term_scr[m] = wr * er + wi * ei
            term_scr[modes + m] = wr * ei - wi * er
    for part in range(2):
        a, b = grad[part][:, :rim], grad[part][:, rim:]
        ra, rb = pltpu.roll(a, half, 1), pltpu.roll(b, half, 1)
        low = lane < half
        lft = jnp.where(first, a, jnp.where(middle, jnp.where(low, 0.0, ra), 0.0))
        own = jnp.where(first, b, jnp.where(middle, jnp.where(low, ra, rb), a))
        rgt = jnp.where(first, 0.0, jnp.where(middle, jnp.where(low, rb, 0.0), b))
        gm[part] = own
        to_near[part] = jnp.where(at.even_col, rgt, lft)
        to_far[part] = jnp.where(at.even_col, lft, rgt)
    if last:
        wr, wi = win_scr[0], win_scr[1]
        term_scr[2 * modes] = wr * wr + wi * wi
        bit = at.j % 2
        each = parts[0].shape[0]
        for k, part in enumerate(parts):
            at = slice((k // 2) * each, (k // 2 + 1) * each)
            offset = (1 - bit if k % 2 else bit) * rim
            part[...] = term_scr[at, pl.ds(pl.multiple_of(offset, rim), rim)]


def fold_body(sizes, sc, gm, near, far, own, to_near, to_far, buf):
    _, _, rows, _, rim = sizes
    at = Place(sc, sizes)
    width = 2 * rim
    buf[...] = jnp.zeros_like(buf)
    buf[:, pl.ds(at.row, width)] = gm[...]
    buf[:, pl.ds(at.near_row, width)] += near[...]
    buf[:, pl.ds(at.far_row_at, width)] += jnp.where(at.far_col, far[...], 0.0)
    top, bottom = buf[:, :rim], buf[:, rim + rows :]
    own[...] = buf[:, rim : rim + rows]
    to_near[...] = jnp.where(at.even_row, bottom, top)
    to_far[...] = jnp.where(at.even_row, top, bottom)


def step_body(sizes, s, own, near, far, denom, out):
    at = Place(None, sizes)
    grad = own[...] + near[...] + jnp.where(at.far_row, far[...], 0.0)
    out[...] = s[...] + grad / denom[...][None]


def leave_body(state, traded, out_re, out_im):
    for k, out in enumerate((out_re, out_im)):
        out[...] = jnp.where(trades(), traded[k], state[k])


def bit_of(axis, level):
    return lax.shift_right_logical(lax.axis_index(("row", "col")[axis]), level) % 2


def halve_body(where, cur, got, keep, send):
    bit = bit_of(*where)
    height = keep.shape[1]
    for out, offset in ((keep, bit * height), (send, (1 - bit) * height)):
        rows = pl.ds(pl.multiple_of(offset, 8), height)
        out[...] = cur[:, rows] + got[:, rows]


def sum_body(cur, got, out):
    out[...] = cur[...] + got[...]


def join_body(where, cur, got, out):
    bit = bit_of(*where)
    height = cur.shape[1]
    for src, offset in ((cur, bit * height), (got, (1 - bit) * height)):
        out[:, pl.ds(pl.multiple_of(offset, 8), height)] = src[...]


def probe_body(rim, *refs):
    colors = (len(refs) - 4) // 2
    mine, got = refs[:colors], refs[colors : 2 * colors]
    pr, pi, new_re, new_im = refs[2 * colors :]
    modes = pr.shape[0]
    each = mine[0].shape[0]
    pixels = 4 * rim * rim
    bit = lax.axis_index("col") % 2

    def term(src, k):
        return src[k // each][k % each]

    mean = (jnp.sum(term(mine, 2 * modes)) + jnp.sum(term(got, 2 * modes))) / pixels
    for src, offset in ((mine, bit * rim), (got, (1 - bit) * rim)):
        rows = pl.ds(pl.multiple_of(offset, rim), rim)
        scale = probe_step / (term(src, 2 * modes) + mass_ratio * mean)
        for m in range(modes):
            new_re[m, rows] = pr[m, rows] + term(src, m) * scale
            new_im[m, rows] = pi[m, rows] + term(src, modes + m) * scale


def swap_bit(array, where):
    axis, level = where
    name = ("row", "col")[axis]
    count = lax.axis_size(name)
    return lax.ppermute(array, name, [(i, i ^ (1 << level)) for i in range(count)])


def sum_terms(keeps, sends, n_row, n_col, beside, late):
    colors = len(keeps)
    each, height, width = keeps[0].shape
    row_bits = [(0, k) for k in range(n_row.bit_length() - 1)]
    col_bits = [(1, k) for k in range(1, n_col.bit_length() - 1)]
    rest = []
    while row_bits or col_bits:
        if row_bits:
            rest.append(row_bits.pop(0))
        if col_bits:
            rest.append(col_bits.pop(0))
    turn = rest[:colors]
    orders = [turn[c:] + turn[:c] for c in range(colors)]
    tail = rest[colors:]
    curs = list(keeps)
    gots = [swap_bit(a, (1, 0)) for a in sends]
    for r in range(len(turn)):
        height //= 2
        for c in range(colors):
            where = orders[c][r]
            outs = [(each, height, width)] * 2
            keep, send = call(functools.partial(halve_body, where), outs)(curs[c], gots[c])
            curs[c], gots[c] = keep, swap_bit(send, where)
        gots = list(beside(r, gots))
    for k, where in enumerate([None] + tail):
        for c in range(colors):
            (curs[c],) = call(sum_body, [curs[c].shape])(curs[c], gots[c])
            if k < len(tail):
                gots[c] = swap_bit(curs[c], tail[k])
    for r in reversed(range(len(turn))):
        for c in range(colors):
            where = orders[c][r]
            got = swap_bit(curs[c], where)
            if c == 0 and r == len(turn) - 2:
                got = late(got)
            outs = [(each, 2 * height, width)]
            (curs[c],) = call(functools.partial(join_body, where), outs)(curs[c], got)
        height *= 2
    return curs, [swap_bit(a, (1, 0)) for a in curs]


def enter_body(n_col, pos, spots):
    at = lax.broadcasted_iota(jnp.int32, spots.shape, 0) * spots.shape[1]
    at = at + lax.broadcasted_iota(jnp.int32, spots.shape, 1)
    me = lax.axis_index("row") * n_col + lax.axis_index("col")
    mine = jnp.where(at == 2 * me, pos[0], jnp.where(at == 2 * me + 1, pos[1], 0))
    spots[...] = mine.astype(F32)


def spot_bits(n_row, n_col):
    bits = [(0, 0)] + [(1, k) for k in range(n_col.bit_length() - 1)]
    return bits + [(0, k) for k in range(1, n_row.bit_length() - 1)]


def gather_spots(known, bits):
    stops = []
    for where in bits:
        known = known + swap_bit(known, where)
        stops.append(known)
    return stops


def local(obj_re, obj_im, probe_re, probe_im, amps, positions):
    rows, cols = obj_re.shape
    modes, width = probe_re.shape[0], probe_re.shape[1]
    rim = width // 2
    n_row, n_col = lax.axis_size("row"), lax.axis_size("col")
    n_dev = n_row * n_col
    sizes = (n_row, n_col, rows, cols, rim)
    tabs = jnp.asarray(tables(width))
    state = jnp.stack([obj_re, obj_im])
    shape = (-(-2 * n_row * n_col // 128), 128)
    (known,) = call(functools.partial(enter_body, n_col), [shape], smem=1)(positions.reshape(2))
    bits = spot_bits(n_row, n_col)
    local_bits = n_col.bit_length()
    stops = gather_spots(known, bits[:local_bits])
    (view,) = call(sort_body, [(width, width)])(amps.reshape(width, width))
    view_raw = view
    probe_re, probe_im, tabs = stage(probe_re, probe_im, tabs)

    grid = (n_row * rows + 2 * rim, n_col * cols + 3 * rim)
    light = call(
        functools.partial(light_body, sizes, n_dev),
        [(rows, cols)],
        [pltpu.VMEM(grid, F32), pltpu.VMEM((2, width, width + rim), F32)],
        1,
        extra=4 << 20,
        cost=pl.CostEstimate(flops=8 * n_dev * width * width, bytes_accessed=10**7, transcendentals=0),
    )

    strip = (2, width, cols)
    tile = (2, rows, cols)
    tall = pltpu.VMEM((2, rows + 2 * rim, cols), F32)
    first_halo = call(functools.partial(first_halo_body, sizes), [(2, rows + 2 * rim, cols), tile])
    halo = call(functools.partial(halo_body, sizes), [strip] * 3, [tall])
    fold = call(functools.partial(fold_body, sizes), [tile] * 3, [tall])
    step = call(functools.partial(step_body, sizes), [tile])
    scratch = [pltpu.VMEM((modes, 2, width, width), F32), pltpu.VMEM((2, width, width), F32)]
    scratch += [pltpu.VMEM((modes * width, width), BF16)] * 2
    scratch += [pltpu.VMEM((modes * width, width), F32)] * 2
    terms = ((2 * modes + 1) // COLORS, rim, width)

    for turn in range(ITERS):
        last = turn == ITERS - 1
        if turn == 0:
            near = swap(state, "row", False)
            far = move(state, row_pairs(n_row, n_col, True, True))
            near, far, sc, view_late = lax.optimization_barrier((near, far, stops[-1], view_raw))
            traded = trade(view_late)
            most = gather_spots(sc, bits[local_bits:-1])[-1]
            mid, state = first_halo(state, near, far)
            to_near = to_far = mid
        else:
            near, far = swap_both(state, state, "row")
            mid, to_near, to_far = halo(sc, state, near, far)
        near, far = swap_both(to_near, to_far, "col")
        if turn == 0:
            near, far, most = lax.optimization_barrier((near, far, most))
            every = gather_spots(most, bits[-1:])[-1]
            (denom,) = light(every.reshape(-1).astype(jnp.int32), probe_re, probe_im)
        outs = [strip] * 3 + ([terms] * 2 * COLORS if last else [])
        scr = scratch + ([pltpu.VMEM((2 * modes + 1, width, width), F32)] if last else [])
        res = call(functools.partial(view_body, sizes, last), outs, scr, extra=8 << 20)(
            sc, mid, near, far, probe_re, probe_im, view, traded, tabs
        )
        gm, to_near, to_far = res[:3]
        near, far = swap_both(to_near, to_far, "col")
        if last:
            break
        own, to_near, to_far = fold(sc, gm, near, far)
        near, far = swap_both(to_near, to_far, "row")
        (state,) = step(state, own, near, far, denom)

    held = {}

    def beside(r, gots):
        if r == 0:
            gots[0], a, b = lax.optimization_barrier((gots[0], near, far))
            held["own"], to_near, to_far = fold(sc, gm, a, b)
            held["both"] = swap_both(to_near, to_far, "row")
        elif r == 1:
            gots[2], a, b = lax.optimization_barrier((gots[2], *held["both"]))
            (held["state"],) = step(state, held["own"], a, b, denom)
            held["traded"] = trade(held["state"])
        return gots

    def late(got):
        got, held["traded"], held["state"] = lax.optimization_barrier(
            (got, held["traded"], held["state"])
        )
        return got

    mine, other = sum_terms(res[3::2], res[4::2], n_row, n_col, beside, late)
    shape = (modes, width, width)
    new_re, new_im = call(functools.partial(probe_body, rim), [shape] * 2)(
        *mine, *other, probe_re, probe_im
    )
    done_re, done_im = call(leave_body, [(rows, cols)] * 2)(held["state"], held["traded"])
    return (done_re, done_im, new_re, new_im)


def solution(mesh):
    placed = (
        P("row", "col"),
        P("row", "col"),
        P(),
        P(),
        P("row", "col", None, None, None),
        P("row", "col", None, None),
    )

    return jax.shard_map(
        local,
        mesh=mesh,
        in_specs=placed,
        out_specs=(P("row", "col"), P("row", "col"), P(), P()),
        check_vma=False,
    )
```

```python
import functools
import math

import jax
import jax.numpy as jnp
import numpy as np
from jax import lax
from jax.experimental import pallas as pl
from jax.experimental.pallas import tpu as pltpu
from jax.sharding import PartitionSpec as P


ITERS = 3

amp_floor = 0.25
light_ratio = 0.1
mass_ratio = 0.1
probe_step = 6.0

F32 = jnp.float32
BF16 = jnp.bfloat16
COLORS = 3


def tables(width):
    half = width // 2
    angle = (np.arange(half)[:, None] * np.arange(width)[None, :] % width) * (2.0 * math.pi / width)
    real = np.cos(angle) / math.sqrt(width)
    imag = -np.sin(angle) / math.sqrt(width)
    pairs = []
    for k in range(2):
        re, im = real[:, k::2], imag[:, k::2]
        pairs.append(np.block([[re, im], [-im, re]]))
    return np.stack(pairs + [p.T for p in pairs]).astype(np.float32).astype(BF16)


def sort_body(view, out):
    width = view.shape[0]
    half = width // 2
    row = lax.broadcasted_iota(jnp.int32, (width, width), 0)
    col = lax.broadcasted_iota(jnp.int32, (width, width), 1)

    def source(k):
        return jnp.where(k < half, 2 * k, 2 * (k - half) + 1)

    def picked(left, rows):
        pick = jnp.where(col == source(row) if rows else row == source(col), 1.0, 0.0).astype(BF16)
        total = jnp.zeros((width, width), F32)
        for _ in range(3):
            part = left.astype(BF16)
            left = left - part.astype(F32)
            pair = (pick, part) if rows else (part, pick)
            total = total + jnp.dot(*pair, preferred_element_type=F32)
        return total

    out[...] = picked(picked(view[...], True), False)


def snake(row):
    return row ^ ((row >> 1) & 1)


def work_row():
    row = lax.axis_index("row")
    return snake(row)


def trades():
    return (lax.axis_index("row") >> 1) % 2 == 1


def across(k, far):
    return (k + 1 if k % 2 else k - 1) if far else k ^ 1


def row_pairs(n_row, n_col, far, stored):
    pairs = []
    for row in range(n_row):
        for j in range(n_col):
            other = across(row, far)
            inside = 0 <= other < n_row
            source = other if inside else row
            source = source if stored else snake(source)
            at = j if inside else j ^ 1
            pairs.append((source * n_col + at, snake(row) * n_col + j))
    return sorted(pairs)


def col_pairs(n_row, n_col, far):
    pairs = []
    for i in range(n_row):
        for j in range(n_col):
            other = across(j, far)
            to = (i, other) if 0 <= other < n_col else (i ^ (2 if n_row % 4 == 0 else 1), j)
            pairs.append((i * n_col + j, to[0] * n_col + to[1]))
    return pairs


def trade_pairs(n_row, n_col):
    pairs = []
    for i in range(n_row):
        for j in range(n_col):
            to = (snake(i), j) if snake(i) != i else (i, j ^ 1)
            pairs.append((i * n_col + j, to[0] * n_col + to[1]))
    return pairs


def move(array, pairs):
    return lax.ppermute(array, ("row", "col"), pairs)


def swap(array, axis, far):
    n_row, n_col = lax.axis_size("row"), lax.axis_size("col")
    if axis == "row":
        return move(array, row_pairs(n_row, n_col, far, False))
    return move(array, col_pairs(n_row, n_col, far))


def trade(array):
    return move(array, trade_pairs(lax.axis_size("row"), lax.axis_size("col")))


def swap_both(to_near, to_far, axis):
    return swap(to_near, axis, False), swap(to_far, axis, True)


def call(body, outs, scratch=(), smem=0, extra=1 << 20, cost=None):
    def run(*args):
        held = sum(4 * math.prod(s) for s in outs) + sum(a.size * a.dtype.itemsize for a in args[smem:])
        held += sum(math.prod(s.shape) * 4 for s in scratch)
        grant = held + extra
        specs = [pl.BlockSpec(memory_space=pltpu.SMEM)] * smem
        specs += [pl.BlockSpec(memory_space=pltpu.VMEM)] * (len(args) - smem)
        return pl.pallas_call(
            body,
            out_shape=[jax.ShapeDtypeStruct(s, F32) for s in outs],
            in_specs=specs,
            out_specs=[pl.BlockSpec(memory_space=pltpu.VMEM)] * len(outs),
            scratch_shapes=list(scratch),
            compiler_params=pltpu.CompilerParams(vmem_limit_bytes=grant),
            cost_estimate=cost,
        )(*args)

    return run


class Place:
    def __init__(self, sc, sizes):
        n_row, n_col, rows, cols, rim = sizes
        self.i, self.j = work_row(), lax.axis_index("col")
        self.even_row = self.i % 2 == 0
        self.even_col = self.j % 2 == 0
        self.up = self.i > 0
        self.down = self.i < n_row - 1
        self.has_left = self.j > 0
        self.has_right = self.j < n_col - 1
        self.far_row = jnp.where(self.even_row, self.i, n_row - 1 - self.i) > 0
        self.far_col = jnp.where(self.even_col, self.j, n_col - 1 - self.j) > 0
        if sc is None:
            return
        near = jnp.where(self.even_col, self.j + 1, self.j - 1)
        far = jnp.where(self.even_col, self.j - 1, self.j + 1)
        far = jnp.where(self.far_col, far, self.j)

        spots = sc[...]
        index = lax.broadcasted_iota(jnp.int32, spots.shape, 0) * spots.shape[1]
        index = index + lax.broadcasted_iota(jnp.int32, spots.shape, 1)

        def known(col, part):
            wanted = 2 * (self.i * n_col + col) + part
            return jnp.sum(jnp.where(index == wanted, spots, 0.0)).astype(jnp.int32)

        def row_of(col):
            return pl.multiple_of(known(col, 0) - (self.i * rows - rim), rim // 2)

        self.row = row_of(self.j)
        self.near_row = row_of(near)
        self.far_row_at = row_of(far)
        self.col = known(self.j, 1) - (self.j * cols - rim)


def light_body(sizes, n_dev, sc, pr, pi, out, buf, pw):
    n_row, n_col, rows, cols, rim = sizes
    width = 2 * rim
    half = rim // 2
    power = jnp.sum(pr[...] * pr[...] + pi[...] * pi[...], axis=0)
    lane = lax.broadcasted_iota(jnp.int32, (width, rim), 1)
    a, b = power[:, :rim], power[:, rim:]
    ra, rb = pltpu.roll(a, half, 1), pltpu.roll(b, half, 1)
    zero = jnp.zeros((width, rim), F32)
    pw[0] = jnp.concatenate([a, b, zero], axis=1)
    pw[1] = jnp.concatenate(
        [jnp.where(lane < half, 0.0, ra), jnp.where(lane < half, ra, rb), jnp.where(lane < half, rb, 0.0)],
        axis=1,
    )
    buf[...] = jnp.zeros_like(buf)

    def add(p, carry):
        row = pl.multiple_of(sc[2 * p] + rim, half)
        col = sc[2 * p + 1] + rim
        odd = (col // half) % 2
        at = (pl.ds(row, width), pl.ds(pl.multiple_of(col - odd * half, rim), width + rim))
        buf[at] += pw[odd]
        return carry

    lax.fori_loop(0, n_dev, add, 0)

    def peak_of(k, best):
        at = pl.multiple_of(k * rows + rim, rim)
        return jnp.maximum(best, jnp.max(buf[pl.ds(at, rows), rim : rim + n_col * cols]))

    peak = lax.fori_loop(0, n_row, peak_of, jnp.float32(0.0))
    mine = buf[
        pl.ds(pl.multiple_of(work_row() * rows + rim, rim), rows),
        pl.ds(pl.multiple_of(lax.axis_index("col") * cols + rim, rim), cols),
    ]
    out[...] = mine + light_ratio * peak


def stage_body(*refs):
    count = len(refs) // 2
    ins, outs, sem = refs[:count], refs[count : 2 * count], refs[2 * count]
    copies = [pltpu.make_async_copy(a, b, sem.at[k]) for k, (a, b) in enumerate(zip(ins, outs))]
    for copy in copies:
        copy.start()
    for copy in copies:
        copy.wait()


def stage(*arrays):
    arrays = [pltpu.with_memory_space_constraint(a, pltpu.HBM) for a in arrays]
    size = sum(a.size * a.dtype.itemsize for a in arrays)
    return pl.pallas_call(
        stage_body,
        out_shape=[jax.ShapeDtypeStruct(a.shape, a.dtype) for a in arrays],
        in_specs=[pl.BlockSpec(memory_space=pltpu.HBM)] * len(arrays),
        out_specs=[pl.BlockSpec(memory_space=pltpu.VMEM)] * len(arrays),
        scratch_shapes=[pltpu.SemaphoreType.DMA((len(arrays),))],
        compiler_params=pltpu.CompilerParams(vmem_limit_bytes=size + (1 << 20)),
        cost_estimate=pl.CostEstimate(flops=0, bytes_accessed=2 * size, transcendentals=0),
    )(*arrays)


def first_halo_body(sizes, s, near, far, out, own):
    _, _, rows, _, rim = sizes
    at = Place(None, sizes)
    here = jnp.where(trades(), near[...], s[...])
    beside = jnp.where(trades(), s[...], near[...])
    above = jnp.where(at.even_row, far[...], beside)
    below = jnp.where(at.even_row, beside, far[...])
    own[...] = here
    out[:, :rim] = jnp.where(at.up, above, 0.0)
    out[:, rim : rim + rows] = here
    out[:, rim + rows :] = jnp.where(at.down, below, 0.0)


def halo_body(sizes, sc, s, near, far, mid, to_near, to_far, ext):
    _, _, rows, _, rim = sizes
    at = Place(sc, sizes)
    width = 2 * rim
    above = jnp.where(at.even_row, far[...], near[...])
    below = jnp.where(at.even_row, near[...], far[...])
    ext[:, :rim] = jnp.where(at.up, above, 0.0)
    ext[:, rim : rim + rows] = s[...]
    ext[:, rim + rows :] = jnp.where(at.down, below, 0.0)
    mid[...] = ext[:, pl.ds(at.row, width)]
    to_near[...] = ext[:, pl.ds(at.near_row, width)]
    to_far[...] = ext[:, pl.ds(at.far_row_at, width)]


def view_body(sizes, last, sc, mid, near, far, pr, pi, view, traded, tabs, *refs):
    if last:
        gm, to_near, to_far, *parts, spec_scr, win_scr, wave_e, wave_o, mix_e, mix_o = refs
    else:
        gm, to_near, to_far, spec_scr, win_scr, wave_e, wave_o, mix_e, mix_o = refs
    _, _, _, _, rim = sizes
    at = Place(sc, sizes)
    modes, width = pr.shape[0], pr.shape[1]
    half = rim // 2
    upper = at.j % 2 == 1

    def put(k, term):
        each = parts[0].shape[0]
        top, low = term[:rim], term[rim:]
        parts[2 * (k // each)][k % each] = jnp.where(upper, low, top)
        parts[2 * (k // each) + 1][k % each] = jnp.where(upper, top, low)

    lane = lax.broadcasted_iota(jnp.int32, (width, rim), 1)
    first = at.col == 0
    middle = at.col == half
    for part in range(2):
        rows_of = pl.ds(at.row, width) if mid.shape[1] > width else slice(None)
        a, b = near[part, rows_of], far[part, rows_of]
        lft = jnp.where(at.has_left, jnp.where(at.even_col, b, a), 0.0)
        rgt = jnp.where(at.has_right, jnp.where(at.even_col, a, b), 0.0)
        own = mid[part, rows_of]
        rl, ro, rr = (pltpu.roll(t, half, 1) for t in (lft, own, rgt))
        win_scr[part, :, :rim] = jnp.where(
            first, lft, jnp.where(middle, jnp.where(lane < half, rl, ro), own)
        )
        win_scr[part, :, rim:] = jnp.where(
            first, own, jnp.where(middle, jnp.where(lane < half, ro, rr), rgt)
        )
    even, odd, even_t, odd_t = range(4)
    for m in range(modes):
        wr, wi = win_scr[0], win_scr[1]
        here = slice(m * width, (m + 1) * width)
        for k, psi in enumerate((pr[m] * wr - pi[m] * wi, pr[m] * wi + pi[m] * wr)):
            lanes = slice(k * rim, (k + 1) * rim)
            wave_e[here, lanes] = (psi[:, :rim] + psi[:, rim:]).astype(BF16)
            wave_o[here, lanes] = (psi[:, :rim] - psi[:, rim:]).astype(BF16)
    mix_e[...] = jnp.dot(wave_e[...], tabs[even], preferred_element_type=F32)
    mix_o[...] = jnp.dot(wave_o[...], tabs[odd], preferred_element_type=F32)
    total = [jnp.zeros((rim, width), F32), jnp.zeros((rim, width), F32)]
    for m in range(modes):
        top, low = slice(m * width, m * width + rim), slice(m * width + rim, (m + 1) * width)
        for k, sign in ((0, 1.0), (1, -1.0)):
            e = mix_e[top] + sign * mix_e[low]
            o = mix_o[top] + sign * mix_o[low]
            tall = jnp.concatenate(
                [
                    jnp.concatenate([e[:, :rim], o[:, :rim]], axis=1),
                    jnp.concatenate([e[:, rim:], o[:, rim:]], axis=1),
                ],
                axis=0,
            ).astype(BF16)
            spec = jnp.dot(tabs[even_t + k], tall, preferred_element_type=F32)
            spec_scr[m, k] = spec
            total[k] = total[k] + (spec[:rim] * spec[:rim] + spec[rim:] * spec[rim:])
    for k in range(2):
        band = slice(k * rim, (k + 1) * rim)
        amps = jnp.where(trades(), traded[band], view[band])
        factor = amps / jnp.maximum(jnp.sqrt(total[k]), amp_floor) - 1.0
        for m in range(modes):
            here = slice((2 * m + k) * rim, (2 * m + k + 1) * rim)
            for part in range(2):
                lanes = slice(part * rim, (part + 1) * rim)
                change = spec_scr[m, k, lanes] * factor
                wave_e[here, lanes] = change[:, :rim].astype(BF16)
                wave_o[here, lanes] = change[:, rim:].astype(BF16)
    mix_e[...] = jnp.dot(wave_e[...], tabs[even_t], preferred_element_type=F32)
    mix_o[...] = jnp.dot(wave_o[...], tabs[odd_t], preferred_element_type=F32)
    grad = [jnp.zeros((width, width), F32), jnp.zeros((width, width), F32)]
    for m in range(modes):
        ends = []
        for k in range(2):
            here = slice((2 * m + k) * rim, (2 * m + k + 1) * rim)
            plus, minus = mix_e[here] + mix_o[here], mix_e[here] - mix_o[here]
            tall = jnp.concatenate(
                [
                    jnp.concatenate([plus[:, :rim], minus[:, :rim]], axis=1),
                    jnp.concatenate([plus[:, rim:], minus[:, rim:]], axis=1),
                ],
                axis=0,
            ).astype(BF16)
            ends.append(jnp.dot(tabs[even + k], tall, preferred_element_type=F32))
        plus, minus = ends[0] + ends[1], ends[0] - ends[1]
        er = jnp.concatenate([plus[:rim], minus[:rim]], axis=0)
        ei = jnp.concatenate([plus[rim:], minus[rim:]], axis=0)
        grad[0] = grad[0] + (pr[m] * er + pi[m] * ei)
        grad[1] = grad[1] + (pr[m] * ei - pi[m] * er)
        if last:
            wr, wi = win_scr[0], win_scr[1]
            put(m, wr * er + wi * ei)
            put(modes + m, wr * ei - wi * er)
    for part in range(2):
        a, b = grad[part][:, :rim], grad[part][:, rim:]
        ra, rb = pltpu.roll(a, half, 1), pltpu.roll(b, half, 1)
        low = lane < half
        lft = jnp.where(first, a, jnp.where(middle, jnp.where(low, 0.0, ra), 0.0))
        own = jnp.where(first, b, jnp.where(middle, jnp.where(low, ra, rb), a))
        rgt = jnp.where(first, 0.0, jnp.where(middle, jnp.where(low, rb, 0.0), b))
        gm[part] = own
        to_near[part] = jnp.where(at.even_col, rgt, lft)
        to_far[part] = jnp.where(at.even_col, lft, rgt)
    if last:
        wr, wi = win_scr[0], win_scr[1]
        put(2 * modes, wr * wr + wi * wi)


def fold_body(sizes, sc, gm, near, far, own, to_near, to_far, buf):
    _, _, rows, _, rim = sizes
    at = Place(sc, sizes)
    width = 2 * rim
    buf[...] = jnp.zeros_like(buf)
    buf[:, pl.ds(at.row, width)] = gm[...]
    buf[:, pl.ds(at.near_row, width)] += near[...]
    buf[:, pl.ds(at.far_row_at, width)] += jnp.where(at.far_col, far[...], 0.0)
    top, bottom = buf[:, :rim], buf[:, rim + rows :]
    own[...] = buf[:, rim : rim + rows]
    to_near[...] = jnp.where(at.even_row, bottom, top)
    to_far[...] = jnp.where(at.even_row, top, bottom)


def step_body(sizes, s, own, near, far, denom, out):
    at = Place(None, sizes)
    grad = own[...] + near[...] + jnp.where(at.far_row, far[...], 0.0)
    out[...] = s[...] + grad / denom[...][None]


def leave_body(state, traded, out_re, out_im):
    for k, out in enumerate((out_re, out_im)):
        out[...] = jnp.where(trades(), traded[k], state[k])


def bit_of(axis, level):
    return lax.shift_right_logical(lax.axis_index(("row", "col")[axis]), level) % 2


def halve_body(where, cur, got, keep, send):
    bit = bit_of(*where)
    height = keep.shape[1]
    for out, offset in ((keep, bit * height), (send, (1 - bit) * height)):
        rows = pl.ds(pl.multiple_of(offset, 8), height)
        out[...] = cur[:, rows] + got[:, rows]


def sum_body(cur, got, out):
    out[...] = cur[...] + got[...]


def join_body(where, cur, got, out):
    bit = bit_of(*where)
    height = cur.shape[1]
    for src, offset in ((cur, bit * height), (got, (1 - bit) * height)):
        out[:, pl.ds(pl.multiple_of(offset, 8), height)] = src[...]


def probe_body(rim, *refs):
    *parts, pr, pi, new_re, new_im, held, sem = refs
    colors = len(parts) // 2
    mine, got = parts[:colors], parts[colors:]
    modes = pr.shape[0]
    each = mine[0].shape[0]
    pixels = 4 * rim * rim
    bit = lax.axis_index("col") % 2

    def term(src, k):
        return src[k // each][k % each]

    mean = (jnp.sum(term(mine, 2 * modes)) + jnp.sum(term(got, 2 * modes))) / pixels
    places = []
    for src, offset in ((mine, bit * rim), (got, (1 - bit) * rim)):
        scale = probe_step / (term(src, 2 * modes) + mass_ratio * mean)
        places.append((src, pl.ds(pl.multiple_of(offset, rim), rim), scale))
    copies = []
    for k, (old, out) in enumerate(((pr, new_re), (pi, new_im))):
        for m in range(modes):
            at = k * modes + m
            for src, rows, scale in places:
                held[at, rows] = old[m, rows] + term(src, at) * scale
            copies.append(pltpu.make_async_copy(held.at[at], out.at[m], sem.at[at]))
            copies[-1].start()
    for copy in copies:
        copy.wait()


def update_probe(rim, parts, pr, pi):
    shape = pr.shape
    both = (2 * shape[0],) + shape[1:]
    size = 4 * (2 * math.prod(both) + sum(p.size for p in parts))
    return pl.pallas_call(
        functools.partial(probe_body, rim),
        out_shape=[jax.ShapeDtypeStruct(shape, F32)] * 2,
        in_specs=[pl.BlockSpec(memory_space=pltpu.VMEM)] * (len(parts) + 2),
        out_specs=[pl.BlockSpec(memory_space=pltpu.HBM)] * 2,
        scratch_shapes=[pltpu.VMEM(both, F32), pltpu.SemaphoreType.DMA((both[0],))],
        compiler_params=pltpu.CompilerParams(vmem_limit_bytes=size + (2 << 20)),
    )(*parts, pr, pi)


def swap_bit(array, where):
    axis, level = where
    name = ("row", "col")[axis]
    count = lax.axis_size(name)
    return lax.ppermute(array, name, [(i, i ^ (1 << level)) for i in range(count)])


def sum_terms(keeps, sends, n_row, n_col, beside, late):
    colors = len(keeps)
    each, height, width = keeps[0].shape
    row_bits = [(0, k) for k in range(n_row.bit_length() - 1)]
    col_bits = [(1, k) for k in range(1, n_col.bit_length() - 1)]
    rest = []
    while row_bits or col_bits:
        if row_bits:
            rest.append(row_bits.pop(0))
        if col_bits:
            rest.append(col_bits.pop(0))
    turn = rest[:colors]
    orders = [turn[c:] + turn[:c] for c in range(colors)]
    tail = rest[colors:]
    curs = list(keeps)
    gots = [swap_bit(a, (1, 0)) for a in sends]
    for r in range(len(turn)):
        height //= 2
        for c in range(colors):
            where = orders[c][r]
            outs = [(each, height, width)] * 2
            keep, send = call(functools.partial(halve_body, where), outs)(curs[c], gots[c])
            curs[c], gots[c] = keep, swap_bit(send, where)
        gots = list(beside(r, gots))
    for k, where in enumerate([None] + tail):
        for c in range(colors):
            (curs[c],) = call(sum_body, [curs[c].shape])(curs[c], gots[c])
            if k < len(tail):
                gots[c] = swap_bit(curs[c], tail[k])
    for r in reversed(range(len(turn))):
        for c in range(colors):
            where = orders[c][r]
            got = swap_bit(curs[c], where)
            if c == 0 and r == len(turn) - 2:
                got = late(got)
            outs = [(each, 2 * height, width)]
            (curs[c],) = call(functools.partial(join_body, where), outs)(curs[c], got)
        height *= 2
    return curs, [swap_bit(a, (1, 0)) for a in curs]


def enter_body(n_col, pos, spots):
    at = lax.broadcasted_iota(jnp.int32, spots.shape, 0) * spots.shape[1]
    at = at + lax.broadcasted_iota(jnp.int32, spots.shape, 1)
    me = lax.axis_index("row") * n_col + lax.axis_index("col")
    mine = jnp.where(at == 2 * me, pos[0], jnp.where(at == 2 * me + 1, pos[1], 0))
    spots[...] = mine.astype(F32)


def spot_bits(n_row, n_col):
    bits = [(0, 0)] + [(1, k) for k in range(n_col.bit_length() - 1)]
    return bits + [(0, k) for k in range(1, n_row.bit_length() - 1)]


def gather_spots(known, bits):
    stops = []
    for where in bits:
        known = known + swap_bit(known, where)
        stops.append(known)
    return stops


def local(obj_re, obj_im, probe_re, probe_im, amps, positions):
    rows, cols = obj_re.shape
    modes, width = probe_re.shape[0], probe_re.shape[1]
    rim = width // 2
    n_row, n_col = lax.axis_size("row"), lax.axis_size("col")
    n_dev = n_row * n_col
    sizes = (n_row, n_col, rows, cols, rim)
    tabs = jnp.asarray(tables(width))
    state = jnp.stack([obj_re, obj_im])
    shape = (-(-2 * n_row * n_col // 128), 128)
    (known,) = call(functools.partial(enter_body, n_col), [shape], smem=1)(positions.reshape(2))
    bits = spot_bits(n_row, n_col)
    local_bits = n_col.bit_length()
    stops = gather_spots(known, bits[:local_bits])
    (view,) = call(sort_body, [(width, width)])(amps.reshape(width, width))
    view_raw = view
    probe_re, probe_im, tabs = stage(probe_re, probe_im, tabs)

    grid = (n_row * rows + 2 * rim, n_col * cols + 3 * rim)
    light = call(
        functools.partial(light_body, sizes, n_dev),
        [(rows, cols)],
        [pltpu.VMEM(grid, F32), pltpu.VMEM((2, width, width + rim), F32)],
        1,
        extra=4 << 20,
        cost=pl.CostEstimate(flops=8 * n_dev * width * width, bytes_accessed=10**7, transcendentals=0),
    )

    strip = (2, width, cols)
    tile = (2, rows, cols)
    tall = pltpu.VMEM((2, rows + 2 * rim, cols), F32)
    first_halo = call(functools.partial(first_halo_body, sizes), [(2, rows + 2 * rim, cols), tile])
    halo = call(functools.partial(halo_body, sizes), [strip] * 3, [tall])
    fold = call(functools.partial(fold_body, sizes), [tile] * 3, [tall])
    step = call(functools.partial(step_body, sizes), [tile])
    scratch = [pltpu.VMEM((modes, 2, width, width), F32), pltpu.VMEM((2, width, width), F32)]
    scratch += [pltpu.VMEM((modes * width, width), BF16)] * 2
    scratch += [pltpu.VMEM((modes * width, width), F32)] * 2
    terms = ((2 * modes + 1) // COLORS, rim, width)

    for turn in range(ITERS):
        last = turn == ITERS - 1
        if turn == 0:
            near = swap(state, "row", False)
            far = move(state, row_pairs(n_row, n_col, True, True))
            near, far, sc, view_late = lax.optimization_barrier((near, far, stops[-1], view_raw))
            traded = trade(view_late)
            most = gather_spots(sc, bits[local_bits:-1])[-1]
            mid, state = first_halo(state, near, far)
            to_near = to_far = mid
        else:
            near, far = swap_both(state, state, "row")
            mid, to_near, to_far = halo(sc, state, near, far)
        near, far = swap_both(to_near, to_far, "col")
        if turn == 0:
            near, far, most = lax.optimization_barrier((near, far, most))
            every = gather_spots(most, bits[-1:])[-1]
            (denom,) = light(every.reshape(-1).astype(jnp.int32), probe_re, probe_im)
        outs = [strip] * 3 + ([terms] * 2 * COLORS if last else [])
        scr = scratch
        res = call(functools.partial(view_body, sizes, last), outs, scr, extra=8 << 20)(
            sc, mid, near, far, probe_re, probe_im, view, traded, tabs
        )
        gm, to_near, to_far = res[:3]
        near, far = swap_both(to_near, to_far, "col")
        if last:
            break
        own, to_near, to_far = fold(sc, gm, near, far)
        near, far = swap_both(to_near, to_far, "row")
        (state,) = step(state, own, near, far, denom)

    held = {}

    def beside(r, gots):
        if r == 0:
            gots[1], a, b = lax.optimization_barrier((gots[1], near, far))
            held["own"], to_near, to_far = fold(sc, gm, a, b)
            held["both"] = swap_both(to_near, to_far, "row")
        elif r == 1:
            gots[2], a, b = lax.optimization_barrier((gots[2], *held["both"]))
            (held["state"],) = step(state, held["own"], a, b, denom)
            held["traded"] = trade(held["state"])
        return gots

    def late(got):
        got, held["traded"], held["state"] = lax.optimization_barrier(
            (got, held["traded"], held["state"])
        )
        return got

    mine, other = sum_terms(res[3::2], res[4::2], n_row, n_col, beside, late)
    new_re, new_im = update_probe(rim, [*mine, *other], probe_re, probe_im)
    done_re, done_im = call(leave_body, [(rows, cols)] * 2)(held["state"], held["traded"])
    return (done_re, done_im, new_re, new_im)


def solution(mesh):
    placed = (
        P("row", "col"),
        P("row", "col"),
        P(),
        P(),
        P("row", "col", None, None, None),
        P("row", "col", None, None),
    )

    return jax.shard_map(
        local,
        mesh=mesh,
        in_specs=placed,
        out_specs=(P("row", "col"), P("row", "col"), P(), P()),
        check_vma=False,
    )
```
